128 devices in a mesh: gx: 16 (over x, z_lo, core), gy: 8 (over z_hi, y).
Axes of the slice: x: 4, y: 4, z: 4 (z_hi: 2, z_lo: 2; z = z_hi * 2 + z_lo), core: 2. Of those that a mesh axis runs over, the one named last changes fastest.
Arguments:
- density: float32 [512, 1024, 256], P('gx', 'gy'), as said below
- reaction_rates: float32 [6], replicated, may hold values from 0.3 to 3
- state_changes: int32 [6, 3], replicated, may hold values from -2 to 2, as said below
- target_box: int32 [2, 3], replicated, may hold values from 0 to 1024, as said below
- truncation: int32 [2], replicated, may hold values from 5 to 16
Outputs:
- occupancy: float32 [512, 1024, 256], P('gx', 'gy')
- summary: float32 [2], replicated
The draws below stay inside these ranges and needn't reach their ends.
Inputs may be any that keep to these rules, and one draw needn't show every extreme that they name: density is positive. `state_changes`: each row is one reaction's change of the three counts; for each of the first two species, some reaction changes it by 2 and some by -2. For each species, target_box[0, d] < target_box[1, d], and target_box[1, d] is at most that species' number of counts; along the species with the most counts the box reaches the lattice's end.
All inputs are finite; a program needn't handle non-finite values.
Results may differ from the reference program's by a relative error of at most 0.0001.
Values sent between devices are 32-bit elements; how exact they have to be, the bound alone decides.
A program may use at most 256 MiB of HBM per device.

```python
import math
import jax
import jax.numpy as jnp
from jax import lax

NZ = 256
STEPS = 4
REACTIONS = 6
NX = 512
NY = 1024


def draw_density(key, part):
    key_first = jax.random.fold_in(key, 0)
    roughness = jnp.exp(jax.random.uniform(key_first, (NX, NY, NZ), jnp.float32, -0.7, 0.7))
    gradient = 1.0 + 2.0 * jnp.arange(NX, dtype=jnp.float32) / (NX - 1)
    return roughness * gradient[:, None, None]


def draw_state_changes(key, part):
    key_list = jax.random.split(key, 3)
    changes = jax.random.randint(key_list[0], (REACTIONS, 3), -2, 3)
    shuffled = jax.random.permutation(key_list[1], REACTIONS)
    direction = 2 * jax.random.randint(key_list[2], (), 0, 2) - 1
    changes = changes.at[shuffled[0], 0].set(2)
    changes = changes.at[shuffled[1], 0].set(-2)
    changes = changes.at[shuffled[2], 1].set(2)
    changes = changes.at[shuffled[3], 1].set(-2)
    changes = changes.at[shuffled[0], 1].set(direction)
    return changes.astype(jnp.int32)


def draw_target_box(key, part):
    key_list = jax.random.split(key, 6)
    extents = (NX, NY, NZ)
    longest = 0
    for axis_number in range(3):
        if extents[axis_number] > extents[longest]:
            longest = axis_number
    lower_bounds = [jax.random.randint(key_list[axis_number], (), 0, extents[axis_number] // 4) for axis_number in range(3)]
    upper_bounds = []
    for axis_number in range(3):
        if axis_number == longest:
            upper_bounds.append(jnp.array(extents[axis_number], jnp.int32))
        else:
            upper_bounds.append(jax.random.randint(key_list[3 + axis_number], (), extents[axis_number] // 2, extents[axis_number] + 1))
    return jnp.stack([jnp.stack(lower_bounds), jnp.stack(upper_bounds)]).astype(jnp.int32)


def setup_inputs(seed: int = 0) -> dict:
    splits = jax.random.split(jax.random.key(seed), 6)
    return {
        "density": draw_density(jax.random.fold_in(splits[5], 71), 0),
        "reaction_rates": jnp.clip(jnp.exp(jax.random.uniform(splits[1], (REACTIONS,), jnp.float32, math.log(0.3), math.log(3.0))), 0.3, 3.0),
        "state_changes": draw_state_changes(jax.random.fold_in(splits[5], 71), 0),
        "target_box": draw_target_box(jax.random.fold_in(splits[5], 71), 0),
        "truncation": jax.random.randint(splits[4], (2,), STEPS + 1, STEPS + 13).astype(jnp.int32),
    }


mean_jumps = 8.0
headroom = 1.05
series_length = 40


def propensity_factor(counts, reactant_order, extent):
    values = counts.astype(jnp.float32)
    linear = values / extent
    square = values * (values - 1.0) / (extent * extent)
    return jnp.where(reactant_order == 0, jnp.ones_like(values), jnp.where(reactant_order == 1, linear, square))


def box_indicator(counts, target_box, axis_number):
    return ((counts >= target_box[0, axis_number]) & (counts < target_box[1, axis_number])).astype(jnp.float32)


def outer_three(along_first, along_second, along_third):
    return along_first[:, None, None] * along_second[None, :, None] * along_third[None, None, :]


def jump_weights(truncation):
    table = [math.exp(-mean_jumps) * mean_jumps ** jump_index / math.factorial(jump_index) for jump_index in range(series_length)]
    weights = [jnp.float32(table[jump_index]) for jump_index in range(STEPS + 1)]
    tails = []
    for which in range(2):
        tail_weight = jnp.float32(0.0)
        for jump_index in range(STEPS + 1, series_length):
            taken = (jump_index <= truncation[which]).astype(jnp.float32)
            tail_weight = tail_weight + taken * jnp.float32(table[jump_index])
        tails.append(tail_weight)
    return weights, tails[0], tails[1]


def reference(density, reaction_rates, state_changes, target_box, truncation):
    extents = (NX, NY, NZ)
    reactant_orders = jnp.maximum(-state_changes, 0)
    count_grids = [jnp.arange(extent, dtype=jnp.int32) for extent in extents]
    inside = [box_indicator(count_grids[axis_number], target_box, axis_number) for axis_number in range(3)]
    box_mask = outer_three(inside[0], inside[1], inside[2])
    factors = [[propensity_factor(count_grids[axis_number], reactant_orders[reaction, axis_number], float(extents[axis_number])) for axis_number in range(3)] for reaction in range(REACTIONS)]
    corner = None
    for reaction in range(REACTIONS):
        corner_term = reaction_rates[reaction]
        for axis_number in range(3):
            last_count = jnp.full((1,), extents[axis_number] - 1, jnp.int32)
            corner_term = corner_term * propensity_factor(last_count, reactant_orders[reaction, axis_number], float(extents[axis_number]))[0]
        corner = corner_term if corner is None else corner + corner_term
    uniform_rate = headroom * corner

    def coefficient(reaction):
        return outer_three(reaction_rates[reaction] * factors[reaction][0], factors[reaction][1], factors[reaction][2])

    total_rate = coefficient(0)
    for reaction in range(1, REACTIONS):
        total_rate = total_rate + coefficient(reaction)

    def advance(current):
        scaled = current * (1.0 - box_mask) / uniform_rate
        advanced = current - total_rate * scaled
        for reaction in range(REACTIONS):
            flux_term = jnp.pad(scaled * coefficient(reaction), 2)
            start = [(2 - state_changes[reaction, axis_number]).astype(jnp.int32) for axis_number in range(3)]
            advanced = advanced + lax.dynamic_slice(flux_term, start, current.shape)
        return advanced

    weights, tail_density, tail_totals = jump_weights(truncation)
    mass_sums = [jnp.sum(density)]
    hit_sums = [jnp.sum(density * box_mask)]
    current = density
    accumulated = weights[0] * density
    for jump_index in range(1, STEPS + 1):
        current = advance(current)
        mass_sums.append(jnp.sum(current))
        hit_sums.append(jnp.sum(current * box_mask))
        accumulated = accumulated + weights[jump_index] * current
    occupancy = accumulated + tail_density * current
    reached = weights[0] * hit_sums[0]
    retained = weights[0] * mass_sums[0]
    for jump_index in range(1, STEPS + 1):
        reached = reached + weights[jump_index] * hit_sums[jump_index]
        retained = retained + weights[jump_index] * mass_sums[jump_index]
    cell_total = float(NX * NY * NZ)
    reached = (reached + tail_totals * hit_sums[STEPS]) / cell_total
    retained = (retained + tail_totals * mass_sums[STEPS]) / cell_total
    return occupancy, jnp.stack([reached, retained])
```

```python
import functools
import math

import jax
import jax.numpy as jnp
from jax import lax
from jax.experimental import pallas as pl
from jax.experimental.pallas import tpu as pltpu
from jax.sharding import PartitionSpec as P

STEPS = 4
mean_jumps = 8.0
headroom = 1.05
series_length = 40
TABLE = [
    math.exp(-mean_jumps) * mean_jumps**k / math.factorial(k) for k in range(series_length)
]
MESH = pl.DeviceIdType.MESH
LANES = 128
PAD = 8
MOVES = [(-1, 0), (1, 0), (0, -1), (0, 1), (-1, -1), (-1, 1), (1, -1), (1, 1)]
BACK = [1, 0, 3, 2, 7, 6, 5, 4]


def quadratic(order, extent):
    zero = jnp.float32(0.0)
    return (
        jnp.where(order == 0, jnp.float32(1.0), zero),
        jnp.where(order == 1, jnp.float32(1.0 / extent), zero),
        jnp.where(order == 2, jnp.float32(1.0 / (extent * extent)), zero),
    )


def evaluate(coefficients, m):
    c0, c1, c2 = coefficients
    return c0 + c1 * m + c2 * (m * (m - 1.0))


def kernel(
    nx, ny, bx, by, reactions,
    density, rates, changes, box, truncation,
    occupancy, summary,
    p, s, d, shifted_b, plain_b, free_table, box_table,
    recv_x, recv_y, recv_c, send_y, send_c, red_y, red_x,
    load_sem, store_sem, send_sem, recv_sem, ysend_sem, yrecv_sem, xsend_sem, xrecv_sem,
):
    me_x, me_y = lax.axis_index("gx"), lax.axis_index("gy")
    anchor_x, anchor_y = me_x * bx, me_y * by
    extents = (nx * bx, ny * by, 2 * LANES)
    yp = by + 2 * PAD
    plane = (bx + 4) * yp

    def present(move):
        px, py = me_x + move[0], me_y + move[1]
        return (px >= 0) & (px < nx) & (py >= 0) & (py < ny)

    exists = [present(move) for move in MOVES]

    loads = [
        pltpu.make_async_copy(
            density.at[:, pl.ds(h * LANES, LANES)], p.at[0, h], load_sem.at[h]
        )
        for h in range(2)
    ]
    for load in loads:
        load.start()

    barrier = pltpu.get_barrier_semaphore()

    def greet(px, py):
        pl.semaphore_signal(barrier, inc=1, device_id=(px, py), device_id_type=MESH)

    @pl.loop(1, nx)
    def _(step):
        greet(lax.rem(me_x + step, nx), me_y)

    @pl.loop(1, ny)
    def _(step):
        greet(me_x, lax.rem(me_y + step, ny))

    corners = jnp.int32(0)
    for way in range(4, 8):
        corners = corners + exists[way].astype(jnp.int32)

        @pl.when(exists[way])
        def _():
            greet(me_x + MOVES[way][0], me_y + MOVES[way][1])

    order = [[jnp.maximum(-changes[r, a], 0) for a in range(3)] for r in range(reactions)]
    phi = [[quadratic(order[r][a], float(extents[a])) for a in range(3)] for r in range(reactions)]
    corner = None
    for r in range(reactions):
        term = rates[r]
        for a in range(3):
            term = term * evaluate(phi[r][a], jnp.float32(extents[a] - 1))
        corner = term if corner is None else corner + term
    inverse_rate = 1.0 / jnp.full((8, LANES), headroom * corner, jnp.float32)
    inverse_rate = inverse_rate[0:1]
    tails = []
    for which in range(2):
        tail = jnp.float32(0.0)
        for k in range(STEPS + 1, series_length):
            tail = tail + jnp.where(k <= truncation[which], jnp.float32(TABLE[k]), jnp.float32(0.0))
        tails.append(tail)
    offsets = [
        (changes[r, 2] + 2) * (2 * plane) + (2 - changes[r, 0]) * yp + (PAD - changes[r, 1])
        for r in range(reactions)
    ]

    def within(count, a):
        return (count >= box[0, a]) & (count < box[1, a])

    def along_x(x_local, move):
        out = []
        for r in range(reactions):
            count = anchor_x + x_local
            if move:
                count = count - changes[r, 0]
            out.append(rates[r] * evaluate(phi[r][0], count.astype(jnp.float32)))
        return out

    def lanes(rows):
        return lax.broadcasted_iota(jnp.int32, (rows, LANES), 1)

    z_count = [lanes(1) + h * LANES for h in range(2)]
    z_float = [z.astype(jnp.float32) for z in z_count]
    z_box = [within(z, 2).astype(jnp.float32) for z in z_count]
    z_one = [z * (1.0 / extents[2]) for z in z_float]
    z_two = [z * (z - 1.0) * (1.0 / extents[2] ** 2) for z in z_float]

    rows = lax.broadcasted_iota(jnp.int32, (by, LANES), 0) + anchor_y
    for r in range(reactions):
        shifted_b[r] = evaluate(phi[r][1], (rows - changes[r, 1]).astype(jnp.float32))
        plain_b[r] = evaluate(phi[r][1], rows.astype(jnp.float32))
    y_box = within(rows, 1).astype(jnp.float32)
    for h in range(2):
        inside = y_box * z_box[h]
        free_table[0, h] = jnp.broadcast_to(inverse_rate, (by, LANES))
        free_table[1, h] = inverse_rate * (1.0 - inside)
        box_table[0, h] = jnp.zeros((by, LANES), jnp.float32)
        box_table[1, h] = inside

    for side, way in ((0, 0), (1, 1)):

        @pl.when(jnp.logical_not(exists[way]))
        def _():
            @pl.loop(0, 10)
            def _(part):
                start = part * plane + (side * (bx + 2)) * yp
                s[pl.ds(pl.multiple_of(start, 8), 2 * yp), :] = jnp.zeros((2 * yp, LANES), jnp.float32)

    for side, way in ((0, 2), (1, 3)):

        @pl.when(jnp.logical_not(exists[way]))
        def _():
            @pl.loop(0, 10 * (bx + 4))
            def _(part):
                start = part * yp + side * (by + PAD)
                s[pl.ds(pl.multiple_of(start, 8), 8), :] = jnp.zeros((8, LANES), jnp.float32)

    for k in range(STEPS):
        for c in range(4):
            send_c[k, c] = jnp.zeros((2, 8, LANES), jnp.float32)

    def halo_copy(k, way):
        px, py = me_x + MOVES[way][0], me_y + MOVES[way][1]
        land = BACK[way]
        if way < 2:
            start = 0 if way == 0 else (bx - 2) * by
            source = p.at[k, :, pl.ds(start, 2 * by), :]
            target = recv_x.at[k, land]
        elif way < 4:
            source = send_y.at[k, way - 2]
            target = recv_y.at[k, land - 2]
        else:
            source = send_c.at[k, way - 4]
            target = recv_c.at[k, land - 4]
        return pltpu.make_async_remote_copy(
            src_ref=source,
            dst_ref=target,
            send_sem=send_sem.at[k, way],
            recv_sem=recv_sem.at[k, land],
            device_id=(px, py),
            device_id_type=MESH,
        )

    def arrived(k, way):
        return pltpu.make_async_remote_copy(
            src_ref=(p.at[k, :, pl.ds(0, 2 * by), :] if way < 2 else send_y.at[k, way - 2] if way < 4 else send_c.at[k, way - 4]),
            dst_ref=(recv_x.at[k, way] if way < 2 else recv_y.at[k, way - 2] if way < 4 else recv_c.at[k, way - 4]),
            send_sem=send_sem.at[k, way],
            recv_sem=recv_sem.at[k, way],
            device_id=(me_x + MOVES[way][0], me_y + MOVES[way][1]),
            device_id_type=MESH,
        )

    def send_faces(k, ways):
        for way in ways:

            @pl.when(exists[way])
            def _():
                halo_copy(k, way).start()

    def pack(k):
        for side in range(2):
            for j in range(2):
                y = j if side == 0 else by - 2 + j
                for h in range(2):
                    send_y[k, side, pl.ds((j * 2 + h) * bx, bx), :] = p[k, h, pl.ds(y, bx, stride=by), :]
        for c in range(4):
            x0 = 0 if MOVES[4 + c][0] < 0 else bx - 2
            y0 = 0 if MOVES[4 + c][1] < 0 else by - 2
            for h in range(2):
                for x in range(2):
                    send_c[k, c, h, pl.ds(2 * x, 2), :] = p[k, h, pl.ds((x0 + x) * by + y0, 2), :]

    def shifts(c0, c1, f0, f1):
        lane = lanes(c0.shape[0])
        zero = jnp.zeros_like(c0)
        a0, a1 = c0 * f0, c1 * f1
        out = []
        for v in range(-2, 3):
            if v == 0:
                out.append((a0, a1))
                continue
            if v > 0:
                t0, t1 = pltpu.roll(a0, v, 1), pltpu.roll(a1, v, 1)
                out.append((jnp.where(lane < v, zero, t0), jnp.where(lane < v, t0, t1)))
            else:
                factor = z_one if v == -1 else z_two
                t0 = pltpu.roll(a0 * factor[0], LANES + v, 1)
                t1 = pltpu.roll(a1 * factor[1], LANES + v, 1)
                edge = lane >= LANES + v
                out.append((jnp.where(edge, t1, t0), jnp.where(edge, zero, t1)))
        return out

    chunk = min(64, by)

    def scale_plane(x_local, load):
        taken = within(anchor_x + x_local, 0).astype(jnp.int32)
        for y0 in range(0, by, chunk):
            c0, c1 = load(0, y0), load(1, y0)
            f0 = free_table[taken, 0, pl.ds(y0, chunk), :]
            f1 = free_table[taken, 1, pl.ds(y0, chunk), :]
            row = pl.multiple_of((x_local + 2) * yp + (PAD + y0), 8)
            for v, pair in enumerate(shifts(c0, c1, f0, f1)):
                for h in range(2):
                    s[pl.ds((v * 2 + h) * plane + row, chunk), :] = pair[h]

    def scale_own(k):
        @pl.loop(0, bx)
        def _(x):
            base = pl.multiple_of(x * by, 8)
            scale_plane(x, lambda h, y0: p[k, h, pl.ds(base + y0, chunk), :])

    def scale_halo(k):
        for way in range(2):

            @pl.when(exists[way])
            def _():
                arrived(k, way).wait_recv()
                for i in range(2):
                    x = i - 2 if way == 0 else bx + i
                    scale_plane(
                        jnp.int32(x),
                        lambda h, y0: recv_x[k, way, h, pl.ds(i * by + y0, chunk), :],
                    )

        x_row = lax.broadcasted_iota(jnp.int32, (bx, LANES), 0) + anchor_x
        x_box = within(x_row, 0).astype(jnp.float32)
        for way in range(2, 4):

            @pl.when(exists[way])
            def _():
                arrived(k, way).wait_recv()
                for j in range(2):
                    y = j - 2 if way == 2 else by + j
                    inside = x_box * within(anchor_y + y, 1).astype(jnp.float32)
                    c0 = recv_y[k, way - 2, pl.ds((j * 2) * bx, bx), :]
                    c1 = recv_y[k, way - 2, pl.ds((j * 2 + 1) * bx, bx), :]
                    f0 = inverse_rate * (1.0 - inside * z_box[0])
                    f1 = inverse_rate * (1.0 - inside * z_box[1])
                    for v, pair in enumerate(shifts(c0, c1, f0, f1)):
                        for h in range(2):
                            s[pl.ds((v * 2 + h) * plane + 2 * yp + PAD + y, bx, stride=yp), :] = pair[h]

        small = lax.broadcasted_iota(jnp.int32, (8, LANES), 0)
        for way in range(4, 8):

            @pl.when(exists[way])
            def _():
                arrived(k, way).wait_recv()
                x0 = -2 if MOVES[way][0] < 0 else bx
                y0 = -2 if MOVES[way][1] < 0 else by
                inside = (
                    within(anchor_x + x0 + (small >> 1), 0) & within(anchor_y + y0 + (small & 1), 1)
                ).astype(jnp.float32)
                c0 = recv_c[k, way - 4, 0]
                c1 = recv_c[k, way - 4, 1]
                f0 = inverse_rate * (1.0 - inside * z_box[0])
                f1 = inverse_rate * (1.0 - inside * z_box[1])
                for v, pair in enumerate(shifts(c0, c1, f0, f1)):
                    for h in range(2):
                        for x in range(2):
                            row = (v * 2 + h) * plane + (x0 + x + 2) * yp + PAD + y0
                            s[pl.ds(row, 2), :] = pair[h][2 * x : 2 * x + 2]

    def advance(k, x, factors, y0, n):
        base = pl.multiple_of(x * by + y0, 8)
        total = [p[k, h, pl.ds(base, n), :] * d[h, pl.ds(base, n), :] for h in range(2)]
        for r in range(reactions):
            along = factors[r] * shifted_b[r, pl.ds(y0, n), :]
            for h in range(2):
                row = offsets[r] + (x * yp + (h * plane + y0))
                total[h] = total[h] + along * s[pl.ds(row, n), :]
        return base, total

    def advance_to(k, x, spans):
        factors = along_x(x, True)
        for y0, n in spans:
            base, total = advance(k, x, factors, y0, n)
            for h in range(2):
                p[k + 1, h, pl.ds(base, n), :] = total[h]

    half = by // 2
    whole = [(0, half), (half, half)]
    inner = (by - 16) // 2
    middle = [(8, inner), (8 + inner, inner)]

    def self_term():
        z_factor = [
            [
                jnp.where(order[r][2] == 0, jnp.ones_like(z_one[h]), jnp.where(order[r][2] == 1, z_one[h], z_two[h]))
                for h in range(2)
            ]
            for r in range(reactions)
        ]

        @pl.loop(0, bx)
        def _(x):
            factors = along_x(x, False)
            taken = within(anchor_x + x, 0).astype(jnp.int32)
            for y0, n in whole:
                total = [None, None]
                for r in range(reactions):
                    along = factors[r] * plain_b[r, pl.ds(y0, n), :]
                    for h in range(2):
                        term = along * z_factor[r][h]
                        total[h] = term if total[h] is None else total[h] + term
                for h in range(2):
                    base = pl.multiple_of(x * by + y0, 8)
                    d[h, pl.ds(base, n), :] = 1.0 - total[h] * free_table[taken, h, pl.ds(y0, n), :]

    for load in loads:
        load.wait()
    pl.semaphore_wait(barrier, nx - 1 + ny - 1 + corners)
    send_faces(0, (0, 1))
    pack(0)
    send_faces(0, range(2, 8))
    scale_own(0)
    self_term()

    @pl.loop(0, STEPS - 1)
    def _(k):
        scale_halo(k)
        for x0 in (0, bx - 2):

            @pl.loop(x0, x0 + 2)
            def _(x):
                advance_to(k, x, whole)

        send_faces(k + 1, (0, 1))

        @pl.loop(2, bx - 2)
        def _(x):
            advance_to(k, x, [(0, 8), (by - 8, 8)])

        pack(k + 1)
        send_faces(k + 1, range(2, 8))

        @pl.loop(2, bx - 2)
        def _(x):
            advance_to(k, x, middle)

        scale_own(k + 1)

    last = STEPS - 1
    scale_halo(last)
    weights = [jnp.float32(TABLE[k]) for k in range(STEPS + 1)]
    weight_density = weights[STEPS] + tails[0]
    weight_total = weights[STEPS] + tails[1]

    def finish(x, carry):
        mass, hit = carry
        factors = along_x(x, True)
        taken = within(anchor_x + x, 0).astype(jnp.int32)
        for y0, n in whole:
            base, total = advance(last, x, factors, y0, n)
            for h in range(2):
                earlier = weights[0] * p[0, h, pl.ds(base, n), :]
                for k in range(1, STEPS):
                    earlier = earlier + weights[k] * p[k, h, pl.ds(base, n), :]
                d[h, pl.ds(base, n), :] = earlier + weight_density * total[h]
                counted = earlier + weight_total * total[h]
                struck = counted * box_table[taken, h, pl.ds(y0, n), :]
                mass = mass + jnp.sum(counted.reshape(n // 8, 8, LANES), axis=0)
                hit = hit + jnp.sum(struck.reshape(n // 8, 8, LANES), axis=0)
        return mass, hit

    zero = jnp.zeros((8, LANES), jnp.float32)
    mass, hit = lax.fori_loop(0, bx, finish, (zero, zero))

    stores = [
        pltpu.make_async_copy(
            d.at[h], occupancy.at[:, pl.ds(h * LANES, LANES)], store_sem.at[h]
        )
        for h in range(2)
    ]
    for store in stores:
        store.start()

    row8 = lax.broadcasted_iota(jnp.int32, (8, LANES), 0)
    red_y[me_y] = jnp.where(
        row8 == 0,
        jnp.sum(mass, axis=0, keepdims=True),
        jnp.where(row8 == 1, jnp.sum(hit, axis=0, keepdims=True), 0.0),
    )

    def share(ref, size, mine, send, recv, device):
        def copy(step, slot):
            return pltpu.make_async_remote_copy(
                src_ref=ref.at[mine],
                dst_ref=ref.at[slot],
                send_sem=send.at[step],
                recv_sem=recv.at[step],
                device_id=device(lax.rem(mine + step, size)),
                device_id_type=MESH,
            )

        @pl.loop(1, size)
        def _(step):
            copy(step, mine).start()

        @pl.loop(1, size)
        def _(step):
            copy(step, lax.rem(mine + size - step, size)).wait_recv()

        @pl.loop(1, size)
        def _(step):
            copy(step, mine).wait_send()

        total = ref[0]
        for slot in range(1, size):
            total = total + ref[slot]
        return total

    red_x[me_x] = share(red_y, ny, me_y, ysend_sem, yrecv_sem, lambda other: (me_x, other))
    total = share(red_x, nx, me_x, xsend_sem, xrecv_sem, lambda other: (other, me_y))
    cells = float(extents[0] * extents[1] * extents[2])
    summary[0] = jnp.sum(total[1:2]) * jnp.float32(1.0 / cells)
    summary[1] = jnp.sum(total[0:1]) * jnp.float32(1.0 / cells)

    for k in range(STEPS):
        for way in range(8):

            @pl.when(exists[way])
            def _():
                halo_copy(k, way).wait_send()

    for store in stores:
        store.wait()


def body(nx, ny, density, reaction_rates, state_changes, target_box, truncation):
    bx, by, nz = density.shape
    reactions = state_changes.shape[0]
    yp = by + 2 * PAD
    f32 = jnp.float32
    vmem = lambda *shape: pltpu.VMEM(shape, f32)
    dma = pltpu.SemaphoreType.DMA
    occupancy, summary = pl.pallas_call(
        functools.partial(kernel, nx, ny, bx, by, reactions),
        out_shape=(
            jax.ShapeDtypeStruct((bx * by, nz), f32),
            jax.ShapeDtypeStruct((2,), f32),
        ),
        in_specs=[pl.BlockSpec(memory_space=pl.ANY)]
        + [pl.BlockSpec(memory_space=pltpu.SMEM)] * 4,
        out_specs=(
            pl.BlockSpec(memory_space=pl.ANY),
            pl.BlockSpec(memory_space=pltpu.SMEM),
        ),
        scratch_shapes=[
            vmem(STEPS, 2, bx * by, LANES),
            vmem(10 * (bx + 4) * yp, LANES),
            vmem(2, bx * by, LANES),
            vmem(reactions, by, LANES),
            vmem(reactions, by, LANES),
            vmem(2, 2, by, LANES),
            vmem(2, 2, by, LANES),
            vmem(STEPS, 2, 2, 2 * by, LANES),
            vmem(STEPS, 2, 4 * bx, LANES),
            vmem(STEPS, 4, 2, 8, LANES),
            vmem(STEPS, 2, 4 * bx, LANES),
            vmem(STEPS, 4, 2, 8, LANES),
            vmem(ny, 8, LANES),
            vmem(nx, 8, LANES),
            dma((2,)),
            dma((2,)),
            dma((STEPS, 8)),
            dma((STEPS, 8)),
            dma((ny,)),
            dma((ny,)),
            dma((nx,)),
            dma((nx,)),
        ],
        compiler_params=pltpu.CompilerParams(
            collective_id=0, has_side_effects=True, vmem_limit_bytes=60 * 1024 * 1024
        ),
    )(density.reshape(bx * by, nz), reaction_rates, state_changes, target_box, truncation)
    return occupancy.reshape(bx, by, nz), summary


def solution(mesh):
    placed = (P("gx", "gy", None), P(), P(), P(), P())
    return jax.shard_map(
        functools.partial(body, mesh.shape["gx"], mesh.shape["gy"]),
        mesh=mesh,
        in_specs=placed,
        out_specs=(P("gx", "gy", None), P()),
        check_vma=False,
    )
```

```python
import functools
import math

import jax
import jax.numpy as jnp
from jax import lax
from jax.experimental import pallas as pl
from jax.experimental.pallas import tpu as pltpu
from jax.sharding import PartitionSpec as P

STEPS = 4
mean_jumps = 8.0
headroom = 1.05
series_length = 40
TABLE = [
    math.exp(-mean_jumps) * mean_jumps**k / math.factorial(k) for k in range(series_length)
]
MESH = pl.DeviceIdType.MESH
LANES = 128
GROUP = 8
MOVED = (1, 2)
PAD = 8
MOVES = [(-1, 0), (1, 0), (0, -1), (0, 1), (-1, -1), (-1, 1), (1, -1), (1, 1)]
BACK = [1, 0, 3, 2, 7, 6, 5, 4]


def quadratic(order, extent):
    zero = jnp.float32(0.0)
    return (
        jnp.where(order == 0, jnp.float32(1.0), zero),
        jnp.where(order == 1, jnp.float32(1.0 / extent), zero),
        jnp.where(order == 2, jnp.float32(1.0 / (extent * extent)), zero),
    )


def evaluate(coefficients, m):
    c0, c1, c2 = coefficients
    return c0 + c1 * m + c2 * (m * (m - 1.0))


def kernel(
    nx, ny, bx, by, reactions,
    density, rates, changes, box, truncation,
    occupancy, summary,
    p, s, d, parts, movers, shifted_b, plain_b, free_table, box_table,
    recv_x, recv_y, recv_c, send_y, send_c, red_y, red_x,
    load_sem, store_sem, send_sem, recv_sem, ysend_sem, yrecv_sem, xsend_sem, xrecv_sem,
):
    me_x, me_y = lax.axis_index("gx"), lax.axis_index("gy")
    anchor_x, anchor_y = me_x * bx, me_y * by
    extents = (nx * bx, ny * by, 2 * LANES)
    yp = by + 2 * PAD
    plane = (bx + 4) * yp

    def present(move):
        px, py = me_x + move[0], me_y + move[1]
        return (px >= 0) & (px < nx) & (py >= 0) & (py < ny)

    exists = [present(move) for move in MOVES]

    loads = [
        pltpu.make_async_copy(
            density.at[:, pl.ds(h * LANES, LANES)], p.at[0, h], load_sem.at[h]
        )
        for h in range(2)
    ]
    for load in loads:
        load.start()

    barrier = pltpu.get_barrier_semaphore()

    def greet(px, py):
        pl.semaphore_signal(barrier, inc=1, device_id=(px, py), device_id_type=MESH)

    @pl.loop(1, nx)
    def _(step):
        greet(lax.rem(me_x + step, nx), me_y)

    @pl.loop(1, ny)
    def _(step):
        greet(me_x, lax.rem(me_y + step, ny))

    corners = jnp.int32(0)
    for way in range(4, 8):
        corners = corners + exists[way].astype(jnp.int32)

        @pl.when(exists[way])
        def _():
            greet(me_x + MOVES[way][0], me_y + MOVES[way][1])

    order = [[jnp.maximum(-changes[a, r], 0) for a in range(3)] for r in range(reactions)]
    phi = [[quadratic(order[r][a], float(extents[a])) for a in range(3)] for r in range(reactions)]
    corner = None
    for r in range(reactions):
        term = rates[r]
        for a in range(3):
            term = term * evaluate(phi[r][a], jnp.float32(extents[a] - 1))
        corner = term if corner is None else corner + term
    inverse_rate = 1.0 / jnp.full((8, LANES), headroom * corner, jnp.float32)
    inverse_rate = inverse_rate[0:1]
    tails = []
    for which in range(2):
        tail = jnp.float32(0.0)
        for k in range(STEPS + 1, series_length):
            tail = tail + jnp.where(k <= truncation[which], jnp.float32(TABLE[k]), jnp.float32(0.0))
        tails.append(tail)
    offsets = [
        (changes[2, r] + 2) * (2 * plane) + (2 - changes[0, r]) * yp + (PAD - changes[1, r])
        for r in range(reactions)
    ]

    def within(count, a):
        return (count >= box[0, a]) & (count < box[1, a])

    def along_x(x_local, move):
        out = []
        for r in range(reactions):
            count = anchor_x + x_local
            if move:
                count = count - changes[0, r]
            out.append(rates[r] * evaluate(phi[r][0], count.astype(jnp.float32)))
        return out

    def lanes(rows):
        return lax.broadcasted_iota(jnp.int32, (rows, LANES), 1)

    z_count = [lanes(1) + h * LANES for h in range(2)]
    z_float = [z.astype(jnp.float32) for z in z_count]
    z_box = [within(z, 2).astype(jnp.float32) for z in z_count]
    z_one = [z * (1.0 / extents[2]) for z in z_float]
    z_two = [z * (z - 1.0) * (1.0 / extents[2] ** 2) for z in z_float]

    z_two_after = [(z + 2.0) * (z + 1.0) * (1.0 / extents[2] ** 2) for z in z_float]
    source = lax.broadcasted_iota(jnp.int32, (4 * LANES, 2 * LANES), 0) & (2 * LANES - 1)
    target = lax.broadcasted_iota(jnp.int32, (4 * LANES, 2 * LANES), 1)
    for m, v in enumerate(MOVED):
        weight = source.astype(jnp.float32) * (1.0 / extents[2]) if v == -1 else jnp.float32(1.0)
        movers[m] = jnp.where(target - source == v, weight, 0.0).astype(jnp.bfloat16)

    rows = lax.broadcasted_iota(jnp.int32, (by, LANES), 0) + anchor_y
    for r in range(reactions):
        shifted_b[r] = evaluate(phi[r][1], (rows - changes[1, r]).astype(jnp.float32))
        plain_b[r] = evaluate(phi[r][1], rows.astype(jnp.float32))
    y_box = within(rows, 1).astype(jnp.float32)
    for h in range(2):
        inside = y_box * z_box[h]
        free_table[0, h] = jnp.broadcast_to(inverse_rate, (by, LANES))
        free_table[1, h] = inverse_rate * (1.0 - inside)
        box_table[0, h] = jnp.zeros((by, LANES), jnp.float32)
        box_table[1, h] = inside

    for side, way in ((0, 0), (1, 1)):

        @pl.when(jnp.logical_not(exists[way]))
        def _():
            @pl.loop(0, 10)
            def _(part):
                start = part * plane + (side * (bx + 2)) * yp
                s[pl.ds(pl.multiple_of(start, 8), 2 * yp), :] = jnp.zeros((2 * yp, LANES), jnp.float32)

    for side, way in ((0, 2), (1, 3)):

        @pl.when(jnp.logical_not(exists[way]))
        def _():
            @pl.loop(0, 10 * (bx + 4))
            def _(part):
                start = part * yp + side * (by + PAD)
                s[pl.ds(pl.multiple_of(start, 8), 8), :] = jnp.zeros((8, LANES), jnp.float32)

    for k in range(STEPS):
        for c in range(4):
            send_c[k, c] = jnp.zeros((2, 8, LANES), jnp.float32)

    def halo_copy(k, way):
        px, py = me_x + MOVES[way][0], me_y + MOVES[way][1]
        land = BACK[way]
        if way < 2:
            start = 0 if way == 0 else (bx - 2) * by
            source = p.at[k, :, pl.ds(start, 2 * by), :]
            target = recv_x.at[k, land]
        elif way < 4:
            source = send_y.at[k, way - 2]
            target = recv_y.at[k, land - 2]
        else:
            source = send_c.at[k, way - 4]
            target = recv_c.at[k, land - 4]
        return pltpu.make_async_remote_copy(
            src_ref=source,
            dst_ref=target,
            send_sem=send_sem.at[k, way],
            recv_sem=recv_sem.at[k, land],
            device_id=(px, py),
            device_id_type=MESH,
        )

    def arrived(k, way):
        return pltpu.make_async_remote_copy(
            src_ref=(p.at[k, :, pl.ds(0, 2 * by), :] if way < 2 else send_y.at[k, way - 2] if way < 4 else send_c.at[k, way - 4]),
            dst_ref=(recv_x.at[k, way] if way < 2 else recv_y.at[k, way - 2] if way < 4 else recv_c.at[k, way - 4]),
            send_sem=send_sem.at[k, way],
            recv_sem=recv_sem.at[k, way],
            device_id=(me_x + MOVES[way][0], me_y + MOVES[way][1]),
            device_id_type=MESH,
        )

    def send_faces(k, ways):
        for way in ways:

            @pl.when(exists[way])
            def _():
                halo_copy(k, way).start()

    def pack(k):
        for side in range(2):
            for j in range(2):
                y = j if side == 0 else by - 2 + j
                for h in range(2):
                    send_y[k, side, pl.ds((j * 2 + h) * bx, bx), :] = p[k, h, pl.ds(y, bx, stride=by), :]
        for c in range(4):
            x0 = 0 if MOVES[4 + c][0] < 0 else bx - 2
            y0 = 0 if MOVES[4 + c][1] < 0 else by - 2
            for h in range(2):
                for x in range(2):
                    send_c[k, c, h, pl.ds(2 * x, 2), :] = p[k, h, pl.ds((x0 + x) * by + y0, 2), :]

    def shifts(c0, c1, f0, f1, skip=()):
        lane = lanes(c0.shape[0])
        zero = jnp.zeros_like(c0)
        a0, a1 = c0 * f0, c1 * f1
        out = []
        for v in range(-2, 3):
            if v == 0:
                out.append((a0, a1))
                continue
            if v in skip:
                out.append(None)
                continue
            if v > 0:
                t0, t1 = pltpu.roll(a0, v, 1), pltpu.roll(a1, v, 1)
                out.append((jnp.where(lane < v, zero, t0), jnp.where(lane < v, t0, t1)))
            else:
                factor = z_one if v == -1 else z_two
                t0 = pltpu.roll(a0 * factor[0], LANES + v, 1)
                t1 = pltpu.roll(a1 * factor[1], LANES + v, 1)
                edge = lane >= LANES + v
                out.append((jnp.where(edge, t1, t0), jnp.where(edge, zero, t1)))
        return out

    chunk = min(64, by)

    def scale_plane(x_local, load, slot=None):
        taken = within(anchor_x + x_local, 0).astype(jnp.int32)
        for y0 in range(0, by, chunk):
            c0, c1 = load(0, y0), load(1, y0)
            f0 = free_table[taken, 0, pl.ds(y0, chunk), :]
            f1 = free_table[taken, 1, pl.ds(y0, chunk), :]
            row = pl.multiple_of((x_local + 2) * yp + (PAD + y0), 8)
            for v, pair in enumerate(shifts(c0, c1, f0, f1, MOVED if slot is not None else ())):
                if pair is None:
                    continue
                for h in range(2):
                    s[pl.ds((v * 2 + h) * plane + row, chunk), :] = pair[h]
                if v == 2 and slot is not None:
                    for h in range(2):
                        high = pair[h].astype(jnp.bfloat16)
                        low = (pair[h] - high.astype(jnp.float32)).astype(jnp.bfloat16)
                        here = pl.ds(slot * by + y0, chunk)
                        parts[here, pl.ds(h * LANES, LANES)] = high
                        parts[here, pl.ds((2 + h) * LANES, LANES)] = low

    def move_planes(x_first, planes):
        for m, v in enumerate(MOVED):
            moved = jnp.dot(
                parts[pl.ds(0, planes * by), :], movers[m], preferred_element_type=jnp.float32
            )
            for h in range(2):
                for i in range(planes):
                    value = moved[i * by : (i + 1) * by, h * LANES : (h + 1) * LANES]
                    if v == -2:
                        value = value * z_two_after[h]
                    row = pl.multiple_of((x_first + i + 2) * yp + PAD, 8)
                    s[pl.ds(((v + 2) * 2 + h) * plane + row, by), :] = value

    def scale_own(k):
        @pl.loop(0, bx // GROUP)
        def _(group):
            first = group * GROUP
            for i in range(GROUP):
                base = pl.multiple_of((first + i) * by, 8)
                scale_plane(first + i, lambda h, y0: p[k, h, pl.ds(base + y0, chunk), :], i)
            move_planes(first, GROUP)

    def scale_halo(k):
        for way in range(2):

            @pl.when(exists[way])
            def _():
                arrived(k, way).wait_recv()
                for i in range(2):
                    x = i - 2 if way == 0 else bx + i
                    scale_plane(
                        jnp.int32(x),
                        lambda h, y0: recv_x[k, way, h, pl.ds(i * by + y0, chunk), :],
                        i,
                    )
                move_planes(-2 if way == 0 else bx, 2)

        x_row = lax.broadcasted_iota(jnp.int32, (bx, LANES), 0) + anchor_x
        x_box = within(x_row, 0).astype(jnp.float32)
        for way in range(2, 4):

            @pl.when(exists[way])
            def _():
                arrived(k, way).wait_recv()
                for j in range(2):
                    y = j - 2 if way == 2 else by + j
                    inside = x_box * within(anchor_y + y, 1).astype(jnp.float32)
                    c0 = recv_y[k, way - 2, pl.ds((j * 2) * bx, bx), :]
                    c1 = recv_y[k, way - 2, pl.ds((j * 2 + 1) * bx, bx), :]
                    f0 = inverse_rate * (1.0 - inside * z_box[0])
                    f1 = inverse_rate * (1.0 - inside * z_box[1])
                    for v, pair in enumerate(shifts(c0, c1, f0, f1)):
                        for h in range(2):
                            s[pl.ds((v * 2 + h) * plane + 2 * yp + PAD + y, bx, stride=yp), :] = pair[h]

        small = lax.broadcasted_iota(jnp.int32, (8, LANES), 0)
        for way in range(4, 8):

            @pl.when(exists[way])
            def _():
                arrived(k, way).wait_recv()
                x0 = -2 if MOVES[way][0] < 0 else bx
                y0 = -2 if MOVES[way][1] < 0 else by
                inside = (
                    within(anchor_x + x0 + (small >> 1), 0) & within(anchor_y + y0 + (small & 1), 1)
                ).astype(jnp.float32)
                c0 = recv_c[k, way - 4, 0]
                c1 = recv_c[k, way - 4, 1]
                f0 = inverse_rate * (1.0 - inside * z_box[0])
                f1 = inverse_rate * (1.0 - inside * z_box[1])
                for v, pair in enumerate(shifts(c0, c1, f0, f1)):
                    for h in range(2):
                        for x in range(2):
                            row = (v * 2 + h) * plane + (x0 + x + 2) * yp + PAD + y0
                            s[pl.ds(row, 2), :] = pair[h][2 * x : 2 * x + 2]

    def advance(k, x, factors, y0, n):
        base = pl.multiple_of(x * by + y0, 8)
        total = [p[k, h, pl.ds(base, n), :] * d[h, pl.ds(base, n), :] for h in range(2)]
        for r in range(reactions):
            along = factors[r] * shifted_b[r, pl.ds(y0, n), :]
            for h in range(2):
                row = offsets[r] + (x * yp + (h * plane + y0))
                total[h] = total[h] + along * s[pl.ds(row, n), :]
        return base, total

    def advance_to(k, x, spans):
        factors = along_x(x, True)
        for y0, n in spans:
            base, total = advance(k, x, factors, y0, n)
            for h in range(2):
                p[k + 1, h, pl.ds(base, n), :] = total[h]

    half = by // 2
    whole = [(0, half), (half, half)]
    inner = (by - 16) // 2
    middle = [(8, inner), (8 + inner, inner)]

    def self_term():
        z_factor = [
            [
                jnp.where(order[r][2] == 0, jnp.ones_like(z_one[h]), jnp.where(order[r][2] == 1, z_one[h], z_two[h]))
                for h in range(2)
            ]
            for r in range(reactions)
        ]

        @pl.loop(0, bx)
        def _(x):
            factors = along_x(x, False)
            taken = within(anchor_x + x, 0).astype(jnp.int32)
            for y0, n in whole:
                total = [None, None]
                for r in range(reactions):
                    along = factors[r] * plain_b[r, pl.ds(y0, n), :]
                    for h in range(2):
                        term = along * z_factor[r][h]
                        total[h] = term if total[h] is None else total[h] + term
                for h in range(2):
                    base = pl.multiple_of(x * by + y0, 8)
                    d[h, pl.ds(base, n), :] = 1.0 - total[h] * free_table[taken, h, pl.ds(y0, n), :]

    for load in loads:
        load.wait()
    pl.semaphore_wait(barrier, nx - 1 + ny - 1 + corners)
    send_faces(0, (0, 1))
    pack(0)
    send_faces(0, range(2, 8))
    scale_own(0)
    self_term()

    @pl.loop(0, STEPS - 1)
    def _(k):
        scale_halo(k)
        for x0 in (0, bx - 2):

            @pl.loop(x0, x0 + 2)
            def _(x):
                advance_to(k, x, whole)

        send_faces(k + 1, (0, 1))

        @pl.loop(2, bx - 2, unroll=4)
        def _(x):
            advance_to(k, x, [(0, 8), (by - 8, 8)])

        pack(k + 1)
        send_faces(k + 1, range(2, 8))

        @pl.loop(2, bx - 2, unroll=2)
        def _(x):
            advance_to(k, x, middle)

        scale_own(k + 1)

    last = STEPS - 1
    scale_halo(last)
    weights = [jnp.float32(TABLE[k]) for k in range(STEPS + 1)]
    weight_density = weights[STEPS] + tails[0]
    weight_total = weights[STEPS] + tails[1]

    def finish(x, carry):
        mass, hit = carry
        factors = along_x(x, True)
        taken = within(anchor_x + x, 0).astype(jnp.int32)
        for y0, n in whole:
            base, total = advance(last, x, factors, y0, n)
            for h in range(2):
                earlier = weights[0] * p[0, h, pl.ds(base, n), :]
                for k in range(1, STEPS):
                    earlier = earlier + weights[k] * p[k, h, pl.ds(base, n), :]
                d[h, pl.ds(base, n), :] = earlier + weight_density * total[h]
                counted = earlier + weight_total * total[h]
                struck = counted * box_table[taken, h, pl.ds(y0, n), :]
                mass = mass + jnp.sum(counted.reshape(n // 8, 8, LANES), axis=0)
                hit = hit + jnp.sum(struck.reshape(n // 8, 8, LANES), axis=0)
        return mass, hit

    zero = jnp.zeros((8, LANES), jnp.float32)
    mass, hit = lax.fori_loop(0, bx, finish, (zero, zero))

    stores = [
        pltpu.make_async_copy(
            d.at[h], occupancy.at[:, pl.ds(h * LANES, LANES)], store_sem.at[h]
        )
        for h in range(2)
    ]
    for store in stores:
        store.start()

    row8 = lax.broadcasted_iota(jnp.int32, (8, LANES), 0)
    red_y[me_y] = jnp.where(
        row8 == 0,
        jnp.sum(mass, axis=0, keepdims=True),
        jnp.where(row8 == 1, jnp.sum(hit, axis=0, keepdims=True), 0.0),
    )

    def share(ref, size, mine, send, recv, device):
        def copy(step, slot):
            return pltpu.make_async_remote_copy(
                src_ref=ref.at[mine],
                dst_ref=ref.at[slot],
                send_sem=send.at[step],
                recv_sem=recv.at[step],
                device_id=device(lax.rem(mine + step, size)),
                device_id_type=MESH,
            )

        @pl.loop(1, size)
        def _(step):
            copy(step, mine).start()

        @pl.loop(1, size)
        def _(step):
            copy(step, lax.rem(mine + size - step, size)).wait_recv()

        @pl.loop(1, size)
        def _(step):
            copy(step, mine).wait_send()

        total = ref[0]
        for slot in range(1, size):
            total = total + ref[slot]
        return total

    red_x[me_x] = share(red_y, ny, me_y, ysend_sem, yrecv_sem, lambda other: (me_x, other))
    total = share(red_x, nx, me_x, xsend_sem, xrecv_sem, lambda other: (other, me_y))
    cells = float(extents[0] * extents[1] * extents[2])
    summary[0] = jnp.sum(total[1:2]) * jnp.float32(1.0 / cells)
    summary[1] = jnp.sum(total[0:1]) * jnp.float32(1.0 / cells)

    for k in range(STEPS):
        for way in range(8):

            @pl.when(exists[way])
            def _():
                halo_copy(k, way).wait_send()

    for store in stores:
        store.wait()


def body(nx, ny, density, reaction_rates, state_changes, target_box, truncation):
    bx, by, nz = density.shape
    reactions = state_changes.shape[0]
    yp = by + 2 * PAD
    f32 = jnp.float32
    vmem = lambda *shape: pltpu.VMEM(shape, f32)
    dma = pltpu.SemaphoreType.DMA
    occupancy, summary = pl.pallas_call(
        functools.partial(kernel, nx, ny, bx, by, reactions),
        out_shape=(
            jax.ShapeDtypeStruct((bx * by, nz), f32),
            jax.ShapeDtypeStruct((2,), f32),
        ),
        in_specs=[pl.BlockSpec(memory_space=pl.ANY)]
        + [pl.BlockSpec(memory_space=pltpu.SMEM)] * 4,
        out_specs=(
            pl.BlockSpec(memory_space=pl.ANY),
            pl.BlockSpec(memory_space=pltpu.SMEM),
        ),
        scratch_shapes=[
            vmem(STEPS, 2, bx * by, LANES),
            vmem(10 * (bx + 4) * yp, LANES),
            vmem(2, bx * by, LANES),
            pltpu.VMEM((GROUP * by, 4 * LANES), jnp.bfloat16),
            pltpu.VMEM((len(MOVED), 4 * LANES, 2 * LANES), jnp.bfloat16),
            vmem(reactions, by, LANES),
            vmem(reactions, by, LANES),
            vmem(2, 2, by, LANES),
            vmem(2, 2, by, LANES),
            vmem(STEPS, 2, 2, 2 * by, LANES),
            vmem(STEPS, 2, 4 * bx, LANES),
            vmem(STEPS, 4, 2, 8, LANES),
            vmem(STEPS, 2, 4 * bx, LANES),
            vmem(STEPS, 4, 2, 8, LANES),
            vmem(ny, 8, LANES),
            vmem(nx, 8, LANES),
            dma((2,)),
            dma((2,)),
            dma((STEPS, 8)),
            dma((STEPS, 8)),
            dma((ny,)),
            dma((ny,)),
            dma((nx,)),
            dma((nx,)),
        ],
        compiler_params=pltpu.CompilerParams(
            collective_id=0, has_side_effects=True, vmem_limit_bytes=60 * 1024 * 1024
        ),
    )(density.reshape(bx * by, nz), reaction_rates, state_changes.T, target_box, truncation)
    return occupancy.reshape(bx, by, nz), summary


def solution(mesh):
    placed = (P("gx", "gy", None), P(), P(), P(), P())
    return jax.shard_map(
        functools.partial(body, mesh.shape["gx"], mesh.shape["gy"]),
        mesh=mesh,
        in_specs=placed,
        out_specs=(P("gx", "gy", None), P()),
        check_vma=False,
    )
```

```python
import functools
import math

import jax
import jax.numpy as jnp
from jax import lax
from jax.experimental import pallas as pl
from jax.experimental.pallas import tpu as pltpu
from jax.sharding import PartitionSpec as P

STEPS = 4
mean_jumps = 8.0
headroom = 1.05
series_length = 40
TABLE = [
    math.exp(-mean_jumps) * mean_jumps**k / math.factorial(k) for k in range(series_length)
]
MESH = pl.DeviceIdType.MESH
LANES = 128
GROUP = 8
MOVED = (1, 2)
PAD = 8
MOVES = [(-1, 0), (1, 0), (0, -1), (0, 1), (-1, -1), (-1, 1), (1, -1), (1, 1)]
BACK = [1, 0, 3, 2, 7, 6, 5, 4]


def quadratic(order, extent):
    zero = jnp.float32(0.0)
    return (
        jnp.where(order == 0, jnp.float32(1.0), zero),
        jnp.where(order == 1, jnp.float32(1.0 / extent), zero),
        jnp.where(order == 2, jnp.float32(1.0 / (extent * extent)), zero),
    )


def evaluate(coefficients, m):
    c0, c1, c2 = coefficients
    return c0 + c1 * m + c2 * (m * (m - 1.0))


def kernel(
    nx, ny, bx, by, reactions,
    density, rates, changes, box, truncation,
    occupancy, summary,
    p, s, d, parts, movers, shifted_b, plain_b, free_table, box_table,
    recv_x, recv_y, recv_c, send_y, send_c, red_y, red_x,
    load_sem, send_sem, recv_sem, ysend_sem, yrecv_sem, xsend_sem, xrecv_sem,
):
    me_x, me_y = lax.axis_index("gx"), lax.axis_index("gy")
    anchor_x, anchor_y = me_x * bx, me_y * by
    extents = (nx * bx, ny * by, 2 * LANES)
    yp = by + 2 * PAD
    plane = (bx + 4) * yp

    def present(move):
        px, py = me_x + move[0], me_y + move[1]
        return (px >= 0) & (px < nx) & (py >= 0) & (py < ny)

    exists = [present(move) for move in MOVES]

    loads = [
        pltpu.make_async_copy(
            density.at[:, pl.ds(h * LANES, LANES)], p.at[0, h], load_sem.at[h]
        )
        for h in range(2)
    ]
    for load in loads:
        load.start()

    barrier = pltpu.get_barrier_semaphore()

    def greet(px, py):
        pl.semaphore_signal(barrier, inc=1, device_id=(px, py), device_id_type=MESH)

    @pl.loop(1, nx)
    def _(step):
        greet(lax.rem(me_x + step, nx), me_y)

    @pl.loop(1, ny)
    def _(step):
        greet(me_x, lax.rem(me_y + step, ny))

    corners = jnp.int32(0)
    for way in range(4, 8):
        corners = corners + exists[way].astype(jnp.int32)

        @pl.when(exists[way])
        def _():
            greet(me_x + MOVES[way][0], me_y + MOVES[way][1])

    for k in range(STEPS):
        for c in range(4):
            send_c[k, c] = jnp.zeros((2, 8, LANES), jnp.float32)

    def halo_copy(k, way):
        px, py = me_x + MOVES[way][0], me_y + MOVES[way][1]
        land = BACK[way]
        if way < 2:
            start = 0 if way == 0 else (bx - 2) * by
            source = p.at[k, :, pl.ds(start, 2 * by), :]
            target = recv_x.at[k, land]
        elif way < 4:
            source = send_y.at[k, way - 2]
            target = recv_y.at[k, land - 2]
        else:
            source = send_c.at[k, way - 4]
            target = recv_c.at[k, land - 4]
        return pltpu.make_async_remote_copy(
            src_ref=source,
            dst_ref=target,
            send_sem=send_sem.at[k, way],
            recv_sem=recv_sem.at[k, land],
            device_id=(px, py),
            device_id_type=MESH,
        )

    def arrived(k, way):
        return pltpu.make_async_remote_copy(
            src_ref=(p.at[k, :, pl.ds(0, 2 * by), :] if way < 2 else send_y.at[k, way - 2] if way < 4 else send_c.at[k, way - 4]),
            dst_ref=(recv_x.at[k, way] if way < 2 else recv_y.at[k, way - 2] if way < 4 else recv_c.at[k, way - 4]),
            send_sem=send_sem.at[k, way],
            recv_sem=recv_sem.at[k, way],
            device_id=(me_x + MOVES[way][0], me_y + MOVES[way][1]),
            device_id_type=MESH,
        )

    def send_faces(k, ways):
        for way in ways:

            @pl.when(exists[way])
            def _():
                halo_copy(k, way).start()

    def pack(k):
        for side in range(2):
            for j in range(2):
                y = j if side == 0 else by - 2 + j
                for h in range(2):
                    send_y[k, side, pl.ds((j * 2 + h) * bx, bx), :] = p[k, h, pl.ds(y, bx, stride=by), :]
        for c in range(4):
            x0 = 0 if MOVES[4 + c][0] < 0 else bx - 2
            y0 = 0 if MOVES[4 + c][1] < 0 else by - 2
            for h in range(2):
                for x in range(2):
                    send_c[k, c, h, pl.ds(2 * x, 2), :] = p[k, h, pl.ds((x0 + x) * by + y0, 2), :]

    for load in loads:
        load.wait()
    pl.semaphore_wait(barrier, nx - 1 + ny - 1 + corners)
    send_faces(0, (0, 1))
    pack(0)
    send_faces(0, range(2, 8))

    order = [[jnp.maximum(-changes[a, r], 0) for a in range(3)] for r in range(reactions)]
    phi = [[quadratic(order[r][a], float(extents[a])) for a in range(3)] for r in range(reactions)]
    corner = None
    for r in range(reactions):
        term = rates[r]
        for a in range(3):
            term = term * evaluate(phi[r][a], jnp.float32(extents[a] - 1))
        corner = term if corner is None else corner + term
    inverse_rate = 1.0 / jnp.full((8, LANES), headroom * corner, jnp.float32)
    inverse_rate = inverse_rate[0:1]
    tails = []
    for which in range(2):
        tail = jnp.float32(0.0)
        for k in range(STEPS + 1, series_length):
            tail = tail + jnp.where(k <= truncation[which], jnp.float32(TABLE[k]), jnp.float32(0.0))
        tails.append(tail)
    offsets = [
        (changes[2, r] + 2) * (2 * plane) + (2 - changes[0, r]) * yp + (PAD - changes[1, r])
        for r in range(reactions)
    ]

    def within(count, a):
        return (count >= box[0, a]) & (count < box[1, a])

    def along_x(x_local, move):
        out = []
        for r in range(reactions):
            count = anchor_x + x_local
            if move:
                count = count - changes[0, r]
            out.append(rates[r] * evaluate(phi[r][0], count.astype(jnp.float32)))
        return out

    def lanes(rows):
        return lax.broadcasted_iota(jnp.int32, (rows, LANES), 1)

    z_count = [lanes(1) + h * LANES for h in range(2)]
    z_float = [z.astype(jnp.float32) for z in z_count]
    z_box = [within(z, 2).astype(jnp.float32) for z in z_count]
    z_one = [z * (1.0 / extents[2]) for z in z_float]
    z_two = [z * (z - 1.0) * (1.0 / extents[2] ** 2) for z in z_float]

    z_two_after = [(z + 2.0) * (z + 1.0) * (1.0 / extents[2] ** 2) for z in z_float]
    source = lax.broadcasted_iota(jnp.int32, (4 * LANES, 2 * LANES), 0) & (2 * LANES - 1)
    target = lax.broadcasted_iota(jnp.int32, (4 * LANES, 2 * LANES), 1)
    for m, v in enumerate(MOVED):
        weight = source.astype(jnp.float32) * (1.0 / extents[2]) if v == -1 else jnp.float32(1.0)
        movers[m] = jnp.where(target - source == v, weight, 0.0).astype(jnp.bfloat16)

    rows = lax.broadcasted_iota(jnp.int32, (by, LANES), 0) + anchor_y
    for r in range(reactions):
        shifted_b[r] = evaluate(phi[r][1], (rows - changes[1, r]).astype(jnp.float32))
        plain_b[r] = evaluate(phi[r][1], rows.astype(jnp.float32))
    y_box = within(rows, 1).astype(jnp.float32)
    for h in range(2):
        inside = y_box * z_box[h]
        free_table[0, h] = jnp.broadcast_to(inverse_rate, (by, LANES))
        free_table[1, h] = inverse_rate * (1.0 - inside)
        box_table[0, h] = jnp.zeros((by, LANES), jnp.float32)
        box_table[1, h] = inside

    for way in range(8):

        @pl.when(jnp.logical_not(exists[way]))
        def _():
            for k in range(STEPS):
                if way < 2:
                    recv_x[k, way] = jnp.zeros((2, 2 * by, LANES), jnp.float32)
                elif way < 4:
                    recv_y[k, way - 2] = jnp.zeros((4 * bx, LANES), jnp.float32)
                else:
                    recv_c[k, way - 4] = jnp.zeros((2, 8, LANES), jnp.float32)

    def shifts(c0, c1, f0, f1, skip=()):
        lane = lanes(c0.shape[0])
        zero = jnp.zeros_like(c0)
        a0, a1 = c0 * f0, c1 * f1
        out = []
        for v in range(-2, 3):
            if v == 0:
                out.append((a0, a1))
                continue
            if v in skip:
                out.append(None)
                continue
            if v > 0:
                t0, t1 = pltpu.roll(a0, v, 1), pltpu.roll(a1, v, 1)
                out.append((jnp.where(lane < v, zero, t0), jnp.where(lane < v, t0, t1)))
            else:
                factor = z_one if v == -1 else z_two
                t0 = pltpu.roll(a0 * factor[0], LANES + v, 1)
                t1 = pltpu.roll(a1 * factor[1], LANES + v, 1)
                edge = lane >= LANES + v
                out.append((jnp.where(edge, t1, t0), jnp.where(edge, zero, t1)))
        return out

    chunk = min(64, by)

    def scale_plane(x_local, load, slot=None):
        taken = within(anchor_x + x_local, 0).astype(jnp.int32)
        for y0 in range(0, by, chunk):
            c0, c1 = load(0, y0), load(1, y0)
            f0 = free_table[taken, 0, pl.ds(y0, chunk), :]
            f1 = free_table[taken, 1, pl.ds(y0, chunk), :]
            row = pl.multiple_of((x_local + 2) * yp + (PAD + y0), 8)
            for v, pair in enumerate(shifts(c0, c1, f0, f1, MOVED if slot is not None else ())):
                if pair is None:
                    continue
                for h in range(2):
                    s[pl.ds((v * 2 + h) * plane + row, chunk), :] = pair[h]
                if v == 2 and slot is not None:
                    for h in range(2):
                        high = pair[h].astype(jnp.bfloat16)
                        low = (pair[h] - high.astype(jnp.float32)).astype(jnp.bfloat16)
                        here = pl.ds(slot * by + y0, chunk)
                        parts[here, pl.ds(h * LANES, LANES)] = high
                        parts[here, pl.ds((2 + h) * LANES, LANES)] = low

    def move_planes(xs):
        for m, v in enumerate(MOVED):
            moved = jnp.dot(
                parts[pl.ds(0, len(xs) * by), :], movers[m], preferred_element_type=jnp.float32
            )
            for h in range(2):
                for i, x in enumerate(xs):
                    value = moved[i * by : (i + 1) * by, h * LANES : (h + 1) * LANES]
                    if v == -2:
                        value = value * z_two_after[h]
                    row = pl.multiple_of((x + 2) * yp + PAD, 8)
                    s[pl.ds(((v + 2) * 2 + h) * plane + row, by), :] = value

    def scale_own(k):
        @pl.loop(0, bx // GROUP)
        def _(group):
            first = group * GROUP
            for i in range(GROUP):
                base = pl.multiple_of((first + i) * by, 8)
                scale_plane(first + i, lambda h, y0: p[k, h, pl.ds(base + y0, chunk), :], i)
            move_planes([first + i for i in range(GROUP)])

    def await_halo(k, ways):
        for way in ways:

            @pl.when(exists[way])
            def _():
                arrived(k, way).wait_recv()

    def scale_halo(k):
        await_halo(k, range(2, 8))
        x_row = lax.broadcasted_iota(jnp.int32, (bx, LANES), 0) + anchor_x
        x_box = within(x_row, 0).astype(jnp.float32)
        for way in range(2, 4):
            for j in range(2):
                y = j - 2 if way == 2 else by + j
                inside = x_box * within(anchor_y + y, 1).astype(jnp.float32)
                c0 = recv_y[k, way - 2, pl.ds((j * 2) * bx, bx), :]
                c1 = recv_y[k, way - 2, pl.ds((j * 2 + 1) * bx, bx), :]
                f0 = inverse_rate * (1.0 - inside * z_box[0])
                f1 = inverse_rate * (1.0 - inside * z_box[1])
                for v, pair in enumerate(shifts(c0, c1, f0, f1)):
                    for h in range(2):
                        s[pl.ds((v * 2 + h) * plane + 2 * yp + PAD + y, bx, stride=yp), :] = pair[h]
        small = lax.broadcasted_iota(jnp.int32, (8, LANES), 0)
        for way in range(4, 8):
            x0 = -2 if MOVES[way][0] < 0 else bx
            y0 = -2 if MOVES[way][1] < 0 else by
            inside = (
                within(anchor_x + x0 + (small >> 1), 0) & within(anchor_y + y0 + (small & 1), 1)
            ).astype(jnp.float32)
            c0 = recv_c[k, way - 4, 0]
            c1 = recv_c[k, way - 4, 1]
            f0 = inverse_rate * (1.0 - inside * z_box[0])
            f1 = inverse_rate * (1.0 - inside * z_box[1])
            for v, pair in enumerate(shifts(c0, c1, f0, f1)):
                for h in range(2):
                    for x in range(2):
                        row = (v * 2 + h) * plane + (x0 + x + 2) * yp + PAD + y0
                        s[pl.ds(row, 2), :] = pair[h][2 * x : 2 * x + 2]
        await_halo(k, range(2))
        places = [(way, i) for way in range(2) for i in range(2)]
        xs = [i - 2 if way == 0 else bx + i for way, i in places]
        for slot, (way, i) in enumerate(places):
            scale_plane(
                jnp.int32(xs[slot]),
                lambda h, y0: recv_x[k, way, h, pl.ds(i * by + y0, chunk), :],
                slot,
            )
        move_planes(xs)

    def advance(k, x, factors, y0, n):
        base = pl.multiple_of(x * by + y0, 8)
        total = [p[k, h, pl.ds(base, n), :] * d[h, pl.ds(base, n), :] for h in range(2)]
        for r in range(reactions):
            along = factors[r] * shifted_b[r, pl.ds(y0, n), :]
            for h in range(2):
                row = offsets[r] + (x * yp + (h * plane + y0))
                total[h] = total[h] + along * s[pl.ds(row, n), :]
        return base, total

    def advance_to(k, x, spans):
        factors = along_x(x, True)
        for y0, n in spans:
            base, total = advance(k, x, factors, y0, n)
            for h in range(2):
                p[k + 1, h, pl.ds(base, n), :] = total[h]

    half = by // 2
    whole = [(0, half), (half, half)]
    inner = (by - 16) // 2
    middle = [(8, inner), (8 + inner, inner)]

    def advance_middle(k):
        @pl.loop(2, bx - 2, unroll=2)
        def _(x):
            advance_to(k, x, middle)

    def self_term():
        z_factor = [
            [
                jnp.where(order[r][2] == 0, jnp.ones_like(z_one[h]), jnp.where(order[r][2] == 1, z_one[h], z_two[h]))
                for h in range(2)
            ]
            for r in range(reactions)
        ]

        @pl.loop(0, bx)
        def _(x):
            factors = along_x(x, False)
            taken = within(anchor_x + x, 0).astype(jnp.int32)
            for y0, n in whole:
                total = [None, None]
                for r in range(reactions):
                    along = factors[r] * plain_b[r, pl.ds(y0, n), :]
                    for h in range(2):
                        term = along * z_factor[r][h]
                        total[h] = term if total[h] is None else total[h] + term
                for h in range(2):
                    base = pl.multiple_of(x * by + y0, 8)
                    d[h, pl.ds(base, n), :] = 1.0 - total[h] * free_table[taken, h, pl.ds(y0, n), :]

    scale_own(0)
    self_term()
    advance_middle(0)

    @pl.loop(0, STEPS - 1)
    def _(k):
        scale_halo(k)
        for x0 in (0, bx - 2):

            @pl.loop(x0, x0 + 2)
            def _(x):
                advance_to(k, x, whole)

        send_faces(k + 1, (0, 1))

        @pl.loop(2, bx - 2, unroll=4)
        def _(x):
            advance_to(k, x, [(0, 8), (by - 8, 8)])

        pack(k + 1)
        send_faces(k + 1, range(2, 8))

        scale_own(k + 1)

        @pl.when(k + 1 < STEPS - 1)
        def _():
            advance_middle(k + 1)

    last = STEPS - 1
    weights = [jnp.float32(TABLE[k]) for k in range(STEPS + 1)]
    weight_density = weights[STEPS] + tails[0]
    weight_total = weights[STEPS] + tails[1]

    def finish(spans, x, carry):
        mass, hit = carry
        factors = along_x(x, True)
        taken = within(anchor_x + x, 0).astype(jnp.int32)
        for y0, n in spans:
            base, total = advance(last, x, factors, y0, n)
            for h in range(2):
                earlier = weights[0] * p[0, h, pl.ds(base, n), :]
                for k in range(1, STEPS):
                    earlier = earlier + weights[k] * p[k, h, pl.ds(base, n), :]
                occupancy[pl.ds(base, n), pl.ds(h * LANES, LANES)] = earlier + weight_density * total[h]
                counted = earlier + weight_total * total[h]
                struck = counted * box_table[taken, h, pl.ds(y0, n), :]
                mass = mass + jnp.sum(counted.reshape(n // 8, 8, LANES), axis=0)
                hit = hit + jnp.sum(struck.reshape(n // 8, 8, LANES), axis=0)
        return mass, hit

    zero = jnp.zeros((8, LANES), jnp.float32)
    sums = lax.fori_loop(2, bx - 2, functools.partial(finish, middle), (zero, zero))
    scale_halo(last)
    for x0 in (0, bx - 2):
        sums = lax.fori_loop(x0, x0 + 2, functools.partial(finish, whole), sums)
    edges = functools.partial(finish, [(0, 8), (by - 8, 8)])
    mass, hit = lax.fori_loop(2, bx - 2, edges, sums, unroll=4)

    row8 = lax.broadcasted_iota(jnp.int32, (8, LANES), 0)
    red_y[me_y] = jnp.where(
        row8 == 0,
        jnp.sum(mass, axis=0, keepdims=True),
        jnp.where(row8 == 1, jnp.sum(hit, axis=0, keepdims=True), 0.0),
    )

    def share_copy(ref, size, mine, send, recv, device, step, slot):
        return pltpu.make_async_remote_copy(
            src_ref=ref.at[mine],
            dst_ref=ref.at[slot],
            send_sem=send.at[step],
            recv_sem=recv.at[step],
            device_id=device(lax.rem(mine + step, size)),
            device_id_type=MESH,
        )

    def share(*group):
        ref, size, mine = group[:3]
        for step in range(1, size):
            share_copy(*group, step, mine).start()
        for step in range(1, size):
            share_copy(*group, step, lax.rem(mine + size - step, size)).wait_recv()
        total = ref[0]
        for slot in range(1, size):
            total = total + ref[slot]
        return total

    along_gy = (red_y, ny, me_y, ysend_sem, yrecv_sem, lambda other: (me_x, other))
    along_gx = (red_x, nx, me_x, xsend_sem, xrecv_sem, lambda other: (other, me_y))
    red_x[me_x] = share(*along_gy)
    total = share(*along_gx)
    cells = float(extents[0] * extents[1] * extents[2])
    summary[0] = jnp.sum(total[1:2]) * jnp.float32(1.0 / cells)
    summary[1] = jnp.sum(total[0:1]) * jnp.float32(1.0 / cells)

    for step in range(1, ny):
        share_copy(*along_gy, step, me_y).wait_send()
    for step in range(1, nx):
        share_copy(*along_gx, step, me_x).wait_send()
    for k in range(STEPS):
        for way in range(8):

            @pl.when(exists[way])
            def _():
                halo_copy(k, way).wait_send()


def body(nx, ny, density, reaction_rates, state_changes, target_box, truncation):
    bx, by, nz = density.shape
    reactions = state_changes.shape[0]
    yp = by + 2 * PAD
    f32 = jnp.float32
    vmem = lambda *shape: pltpu.VMEM(shape, f32)
    dma = pltpu.SemaphoreType.DMA
    occupancy, summary = pl.pallas_call(
        functools.partial(kernel, nx, ny, bx, by, reactions),
        out_shape=(
            pltpu.VMEM((bx * by, nz), f32),
            jax.ShapeDtypeStruct((2,), f32),
        ),
        in_specs=[pl.BlockSpec(memory_space=pl.ANY)]
        + [pl.BlockSpec(memory_space=pltpu.SMEM)] * 4,
        out_specs=(
            pl.BlockSpec(memory_space=pltpu.VMEM),
            pl.BlockSpec(memory_space=pltpu.SMEM),
        ),
        scratch_shapes=[
            vmem(STEPS, 2, bx * by, LANES),
            vmem(10 * (bx + 4) * yp, LANES),
            vmem(2, bx * by, LANES),
            pltpu.VMEM((GROUP * by, 4 * LANES), jnp.bfloat16),
            pltpu.VMEM((len(MOVED), 4 * LANES, 2 * LANES), jnp.bfloat16),
            vmem(reactions, by, LANES),
            vmem(reactions, by, LANES),
            vmem(2, 2, by, LANES),
            vmem(2, 2, by, LANES),
            vmem(STEPS, 2, 2, 2 * by, LANES),
            vmem(STEPS, 2, 4 * bx, LANES),
            vmem(STEPS, 4, 2, 8, LANES),
            vmem(STEPS, 2, 4 * bx, LANES),
            vmem(STEPS, 4, 2, 8, LANES),
            vmem(ny, 8, LANES),
            vmem(nx, 8, LANES),
            dma((2,)),
            dma((STEPS, 8)),
            dma((STEPS, 8)),
            dma((ny,)),
            dma((ny,)),
            dma((nx,)),
            dma((nx,)),
        ],
        compiler_params=pltpu.CompilerParams(
            collective_id=0, has_side_effects=True, vmem_limit_bytes=54 * 1024 * 1024
        ),
    )(density.reshape(bx * by, nz), reaction_rates, state_changes.T, target_box, truncation)
    return occupancy.reshape(bx, by, nz), summary


def solution(mesh):
    placed = (P("gx", "gy", None), P(), P(), P(), P())
    return jax.shard_map(
        functools.partial(body, mesh.shape["gx"], mesh.shape["gy"]),
        mesh=mesh,
        in_specs=placed,
        out_specs=(P("gx", "gy", None), P()),
        check_vma=False,
    )
```

```python
import functools
import math

import jax
import jax.numpy as jnp
from jax import lax
from jax.experimental import pallas as pl
from jax.experimental.pallas import tpu as pltpu
from jax.sharding import PartitionSpec as P

STEPS = 4
mean_jumps = 8.0
headroom = 1.05
series_length = 40
TABLE = [
    math.exp(-mean_jumps) * mean_jumps**k / math.factorial(k) for k in range(series_length)
]
MESH = pl.DeviceIdType.MESH
LANES = 128
GROUP = 8
MOVED = (1, 2)
PAD = 8
MOVES = [(-1, 0), (1, 0), (0, -1), (0, 1), (-1, -1), (-1, 1), (1, -1), (1, 1)]
BACK = [1, 0, 3, 2, 7, 6, 5, 4]


def quadratic(order, extent):
    zero = jnp.float32(0.0)
    return (
        jnp.where(order == 0, jnp.float32(1.0), zero),
        jnp.where(order == 1, jnp.float32(1.0 / extent), zero),
        jnp.where(order == 2, jnp.float32(1.0 / (extent * extent)), zero),
    )


def evaluate(coefficients, m):
    c0, c1, c2 = coefficients
    return c0 + c1 * m + c2 * (m * (m - 1.0))


def kernel(
    nx, ny, bx, by, reactions,
    density, rates, changes, box, truncation,
    occupancy, summary,
    p, s, d, parts, movers, shifted_b, plain_b, free_table, box_table,
    recv_x, recv_y, recv_c, send_y, send_c, red_near, red_far,
    load_sem, send_sem, recv_sem, nsend_sem, nrecv_sem, fsend_sem, frecv_sem,
):
    me_x, me_y = lax.axis_index("gx"), lax.axis_index("gy")
    anchor_x, anchor_y = me_x * bx, me_y * by
    extents = (nx * bx, ny * by, 2 * LANES)
    yp = by + 2 * PAD
    plane = (bx + 4) * yp

    def present(move):
        px, py = me_x + move[0], me_y + move[1]
        return (px >= 0) & (px < nx) & (py >= 0) & (py < ny)

    exists = [present(move) for move in MOVES]

    loads = [
        pltpu.make_async_copy(
            density.at[:, pl.ds(h * LANES, LANES)], p.at[0, h], load_sem.at[h]
        )
        for h in range(2)
    ]
    for load in loads:
        load.start()

    barrier = pltpu.get_barrier_semaphore()

    def greet(px, py):
        pl.semaphore_signal(barrier, inc=1, device_id=(px, py), device_id_type=MESH)

    inner_x, outer_y = 4, 2
    outer_x, inner_y = nx // inner_x, ny // outer_y
    near_size, far_size = inner_x * outer_y, outer_x * inner_y
    near_me = (me_x % inner_x) * outer_y + me_y // inner_y
    far_me = (me_x // inner_x) * inner_y + me_y % inner_y

    def near_device(other):
        return (
            (me_x // inner_x) * inner_x + other // outer_y,
            (other % outer_y) * inner_y + me_y % inner_y,
        )

    def far_device(other):
        return (
            (other // inner_y) * inner_x + me_x % inner_x,
            (me_y // inner_y) * inner_y + other % inner_y,
        )

    for size, mine, device in ((near_size, near_me, near_device), (far_size, far_me, far_device)):

        @pl.loop(1, size)
        def _(step):
            greet(*device((mine + step) % size))

    others = jnp.int32(0)
    for way in range(8):
        px, py = me_x + MOVES[way][0], me_y + MOVES[way][1]
        is_near = (px // inner_x == me_x // inner_x) & (py % inner_y == me_y % inner_y)
        is_far = (px % inner_x == me_x % inner_x) & (py // inner_y == me_y // inner_y)
        alone = exists[way] & jnp.logical_not(is_near | is_far)
        others = others + alone.astype(jnp.int32)

        @pl.when(alone)
        def _():
            greet(px, py)

    for k in range(STEPS):
        for c in range(4):
            send_c[k, c] = jnp.zeros((2, 8, LANES), jnp.float32)

    def halo_copy(k, way):
        px, py = me_x + MOVES[way][0], me_y + MOVES[way][1]
        land = BACK[way]
        if way < 2:
            start = 0 if way == 0 else (bx - 2) * by
            source = p.at[k, :, pl.ds(start, 2 * by), :]
            target = recv_x.at[k, land]
        elif way < 4:
            source = send_y.at[k, way - 2]
            target = recv_y.at[k, land - 2]
        else:
            source = send_c.at[k, way - 4]
            target = recv_c.at[k, land - 4]
        return pltpu.make_async_remote_copy(
            src_ref=source,
            dst_ref=target,
            send_sem=send_sem.at[k, way],
            recv_sem=recv_sem.at[k, land],
            device_id=(px, py),
            device_id_type=MESH,
        )

    def arrived(k, way):
        return pltpu.make_async_remote_copy(
            src_ref=(p.at[k, :, pl.ds(0, 2 * by), :] if way < 2 else send_y.at[k, way - 2] if way < 4 else send_c.at[k, way - 4]),
            dst_ref=(recv_x.at[k, way] if way < 2 else recv_y.at[k, way - 2] if way < 4 else recv_c.at[k, way - 4]),
            send_sem=send_sem.at[k, way],
            recv_sem=recv_sem.at[k, way],
            device_id=(me_x + MOVES[way][0], me_y + MOVES[way][1]),
            device_id_type=MESH,
        )

    def send_faces(k, ways):
        for way in ways:

            @pl.when(exists[way])
            def _():
                halo_copy(k, way).start()

    def pack(k):
        for side in range(2):
            for j in range(2):
                y = j if side == 0 else by - 2 + j
                for h in range(2):
                    send_y[k, side, pl.ds((j * 2 + h) * bx, bx), :] = p[k, h, pl.ds(y, bx, stride=by), :]
        for c in range(4):
            x0 = 0 if MOVES[4 + c][0] < 0 else bx - 2
            y0 = 0 if MOVES[4 + c][1] < 0 else by - 2
            for h in range(2):
                for x in range(2):
                    send_c[k, c, h, pl.ds(2 * x, 2), :] = p[k, h, pl.ds((x0 + x) * by + y0, 2), :]

    for load in loads:
        load.wait()
    pl.semaphore_wait(barrier, near_size - 1 + far_size - 1 + others)
    send_faces(0, (0, 1))
    pack(0)
    send_faces(0, range(2, 8))

    order = [[jnp.maximum(-changes[a, r], 0) for a in range(3)] for r in range(reactions)]
    phi = [[quadratic(order[r][a], float(extents[a])) for a in range(3)] for r in range(reactions)]
    corner = None
    for r in range(reactions):
        term = rates[r]
        for a in range(3):
            term = term * evaluate(phi[r][a], jnp.float32(extents[a] - 1))
        corner = term if corner is None else corner + term
    inverse_rate = 1.0 / jnp.full((8, LANES), headroom * corner, jnp.float32)
    inverse_rate = inverse_rate[0:1]
    tails = []
    for which in range(2):
        tail = jnp.float32(0.0)
        for k in range(STEPS + 1, series_length):
            tail = tail + jnp.where(k <= truncation[which], jnp.float32(TABLE[k]), jnp.float32(0.0))
        tails.append(tail)
    offsets = [
        (changes[2, r] + 2) * (2 * plane) + (2 - changes[0, r]) * yp + (PAD - changes[1, r])
        for r in range(reactions)
    ]

    def within(count, a):
        return (count >= box[0, a]) & (count < box[1, a])

    def along_x(x_local, move):
        out = []
        for r in range(reactions):
            count = anchor_x + x_local
            if move:
                count = count - changes[0, r]
            out.append(rates[r] * evaluate(phi[r][0], count.astype(jnp.float32)))
        return out

    def lanes(rows):
        return lax.broadcasted_iota(jnp.int32, (rows, LANES), 1)

    z_count = [lanes(1) + h * LANES for h in range(2)]
    z_float = [z.astype(jnp.float32) for z in z_count]
    z_box = [within(z, 2).astype(jnp.float32) for z in z_count]
    z_one = [z * (1.0 / extents[2]) for z in z_float]
    z_two = [z * (z - 1.0) * (1.0 / extents[2] ** 2) for z in z_float]

    z_two_after = [(z + 2.0) * (z + 1.0) * (1.0 / extents[2] ** 2) for z in z_float]
    source = lax.broadcasted_iota(jnp.int32, (4 * LANES, 2 * LANES), 0) & (2 * LANES - 1)
    target = lax.broadcasted_iota(jnp.int32, (4 * LANES, 2 * LANES), 1)
    for m, v in enumerate(MOVED):
        weight = source.astype(jnp.float32) * (1.0 / extents[2]) if v == -1 else jnp.float32(1.0)
        movers[m] = jnp.where(target - source == v, weight, 0.0).astype(jnp.bfloat16)

    rows = lax.broadcasted_iota(jnp.int32, (by, LANES), 0) + anchor_y
    for r in range(reactions):
        shifted_b[r] = evaluate(phi[r][1], (rows - changes[1, r]).astype(jnp.float32))
        plain_b[r] = evaluate(phi[r][1], rows.astype(jnp.float32))
    y_box = within(rows, 1).astype(jnp.float32)
    for h in range(2):
        inside = y_box * z_box[h]
        free_table[0, h] = jnp.broadcast_to(inverse_rate, (by, LANES))
        free_table[1, h] = inverse_rate * (1.0 - inside)
        box_table[0, h] = jnp.zeros((by, LANES), jnp.float32)
        box_table[1, h] = inside

    for way in range(8):

        @pl.when(jnp.logical_not(exists[way]))
        def _():
            for k in range(STEPS):
                if way < 2:
                    recv_x[k, way] = jnp.zeros((2, 2 * by, LANES), jnp.float32)
                elif way < 4:
                    recv_y[k, way - 2] = jnp.zeros((4 * bx, LANES), jnp.float32)
                else:
                    recv_c[k, way - 4] = jnp.zeros((2, 8, LANES), jnp.float32)

    def shifts(c0, c1, f0, f1, skip=()):
        lane = lanes(c0.shape[0])
        zero = jnp.zeros_like(c0)
        a0, a1 = c0 * f0, c1 * f1
        out = []
        for v in range(-2, 3):
            if v == 0:
                out.append((a0, a1))
                continue
            if v in skip:
                out.append(None)
                continue
            if v > 0:
                t0, t1 = pltpu.roll(a0, v, 1), pltpu.roll(a1, v, 1)
                out.append((jnp.where(lane < v, zero, t0), jnp.where(lane < v, t0, t1)))
            else:
                factor = z_one if v == -1 else z_two
                t0 = pltpu.roll(a0 * factor[0], LANES + v, 1)
                t1 = pltpu.roll(a1 * factor[1], LANES + v, 1)
                edge = lane >= LANES + v
                out.append((jnp.where(edge, t1, t0), jnp.where(edge, zero, t1)))
        return out

    chunk = min(64, by)

    def scale_plane(x_local, load, slot=None):
        taken = within(anchor_x + x_local, 0).astype(jnp.int32)
        for y0 in range(0, by, chunk):
            c0, c1 = load(0, y0), load(1, y0)
            f0 = free_table[taken, 0, pl.ds(y0, chunk), :]
            f1 = free_table[taken, 1, pl.ds(y0, chunk), :]
            row = pl.multiple_of((x_local + 2) * yp + (PAD + y0), 8)
            for v, pair in enumerate(shifts(c0, c1, f0, f1, MOVED if slot is not None else ())):
                if pair is None:
                    continue
                for h in range(2):
                    s[pl.ds((v * 2 + h) * plane + row, chunk), :] = pair[h]
                if v == 2 and slot is not None:
                    for h in range(2):
                        high = pair[h].astype(jnp.bfloat16)
                        low = (pair[h] - high.astype(jnp.float32)).astype(jnp.bfloat16)
                        here = pl.ds(slot * by + y0, chunk)
                        parts[here, pl.ds(h * LANES, LANES)] = high
                        parts[here, pl.ds((2 + h) * LANES, LANES)] = low

    def move_planes(xs):
        for m, v in enumerate(MOVED):
            moved = jnp.dot(
                parts[pl.ds(0, len(xs) * by), :], movers[m], preferred_element_type=jnp.float32
            )
            for h in range(2):
                for i, x in enumerate(xs):
                    value = moved[i * by : (i + 1) * by, h * LANES : (h + 1) * LANES]
                    if v == -2:
                        value = value * z_two_after[h]
                    row = pl.multiple_of((x + 2) * yp + PAD, 8)
                    s[pl.ds(((v + 2) * 2 + h) * plane + row, by), :] = value

    def scale_own(k):
        @pl.loop(0, bx // GROUP)
        def _(group):
            first = group * GROUP
            for i in range(GROUP):
                base = pl.multiple_of((first + i) * by, 8)
                scale_plane(first + i, lambda h, y0: p[k, h, pl.ds(base + y0, chunk), :], i)
            move_planes([first + i for i in range(GROUP)])

    def await_halo(k, ways):
        for way in ways:

            @pl.when(exists[way])
            def _():
                arrived(k, way).wait_recv()

    def scale_halo(k):
        await_halo(k, range(2, 8))
        x_row = lax.broadcasted_iota(jnp.int32, (bx, LANES), 0) + anchor_x
        x_box = within(x_row, 0).astype(jnp.float32)
        for way in range(2, 4):
            for j in range(2):
                y = j - 2 if way == 2 else by + j
                inside = x_box * within(anchor_y + y, 1).astype(jnp.float32)
                c0 = recv_y[k, way - 2, pl.ds((j * 2) * bx, bx), :]
                c1 = recv_y[k, way - 2, pl.ds((j * 2 + 1) * bx, bx), :]
                f0 = inverse_rate * (1.0 - inside * z_box[0])
                f1 = inverse_rate * (1.0 - inside * z_box[1])
                for v, pair in enumerate(shifts(c0, c1, f0, f1)):
                    for h in range(2):
                        s[pl.ds((v * 2 + h) * plane + 2 * yp + PAD + y, bx, stride=yp), :] = pair[h]
        small = lax.broadcasted_iota(jnp.int32, (8, LANES), 0)
        for way in range(4, 8):
            x0 = -2 if MOVES[way][0] < 0 else bx
            y0 = -2 if MOVES[way][1] < 0 else by
            inside = (
                within(anchor_x + x0 + (small >> 1), 0) & within(anchor_y + y0 + (small & 1), 1)
            ).astype(jnp.float32)
            c0 = recv_c[k, way - 4, 0]
            c1 = recv_c[k, way - 4, 1]
            f0 = inverse_rate * (1.0 - inside * z_box[0])
            f1 = inverse_rate * (1.0 - inside * z_box[1])
            for v, pair in enumerate(shifts(c0, c1, f0, f1)):
                for h in range(2):
                    for x in range(2):
                        row = (v * 2 + h) * plane + (x0 + x + 2) * yp + PAD + y0
                        s[pl.ds(row, 2), :] = pair[h][2 * x : 2 * x + 2]
        await_halo(k, range(2))
        places = [(way, i) for way in range(2) for i in range(2)]
        xs = [i - 2 if way == 0 else bx + i for way, i in places]
        for slot, (way, i) in enumerate(places):
            scale_plane(
                jnp.int32(xs[slot]),
                lambda h, y0: recv_x[k, way, h, pl.ds(i * by + y0, chunk), :],
                slot,
            )
        move_planes(xs)

    def advance(k, x, factors, y0, n):
        base = pl.multiple_of(x * by + y0, 8)
        total = [p[k, h, pl.ds(base, n), :] * d[h, pl.ds(base, n), :] for h in range(2)]
        for r in range(reactions):
            along = factors[r] * shifted_b[r, pl.ds(y0, n), :]
            for h in range(2):
                row = offsets[r] + (x * yp + (h * plane + y0))
                total[h] = total[h] + along * s[pl.ds(row, n), :]
        return base, total

    def advance_to(k, x, spans):
        factors = along_x(x, True)
        for y0, n in spans:
            base, total = advance(k, x, factors, y0, n)
            for h in range(2):
                p[k + 1, h, pl.ds(base, n), :] = total[h]

    half = by // 2
    whole = [(0, half), (half, half)]
    inner = (by - 16) // 2
    middle = [(8, inner), (8 + inner, inner)]

    def advance_middle(k):
        @pl.loop(2, bx - 2, unroll=2)
        def _(x):
            advance_to(k, x, middle)

    def self_term():
        z_factor = [
            [
                jnp.where(order[r][2] == 0, jnp.ones_like(z_one[h]), jnp.where(order[r][2] == 1, z_one[h], z_two[h]))
                for h in range(2)
            ]
            for r in range(reactions)
        ]

        @pl.loop(0, bx)
        def _(x):
            factors = along_x(x, False)
            taken = within(anchor_x + x, 0).astype(jnp.int32)
            for y0, n in whole:
                total = [None, None]
                for r in range(reactions):
                    along = factors[r] * plain_b[r, pl.ds(y0, n), :]
                    for h in range(2):
                        term = along * z_factor[r][h]
                        total[h] = term if total[h] is None else total[h] + term
                for h in range(2):
                    base = pl.multiple_of(x * by + y0, 8)
                    d[h, pl.ds(base, n), :] = 1.0 - total[h] * free_table[taken, h, pl.ds(y0, n), :]

    scale_own(0)
    self_term()
    advance_middle(0)

    @pl.loop(0, STEPS - 1)
    def _(k):
        scale_halo(k)
        for x0 in (0, bx - 2):

            @pl.loop(x0, x0 + 2)
            def _(x):
                advance_to(k, x, whole)

        send_faces(k + 1, (0, 1))

        @pl.loop(2, bx - 2, unroll=4)
        def _(x):
            advance_to(k, x, [(0, 8), (by - 8, 8)])

        pack(k + 1)
        send_faces(k + 1, range(2, 8))

        scale_own(k + 1)

        @pl.when(k + 1 < STEPS - 1)
        def _():
            advance_middle(k + 1)

    last = STEPS - 1
    weights = [jnp.float32(TABLE[k]) for k in range(STEPS + 1)]
    weight_density = weights[STEPS] + tails[0]
    weight_total = weights[STEPS] + tails[1]

    def finish(spans, x, carry):
        mass, hit = carry
        factors = along_x(x, True)
        taken = within(anchor_x + x, 0).astype(jnp.int32)
        for y0, n in spans:
            base, total = advance(last, x, factors, y0, n)
            for h in range(2):
                earlier = weights[0] * p[0, h, pl.ds(base, n), :]
                for k in range(1, STEPS):
                    earlier = earlier + weights[k] * p[k, h, pl.ds(base, n), :]
                occupancy[pl.ds(base, n), pl.ds(h * LANES, LANES)] = earlier + weight_density * total[h]
                counted = earlier + weight_total * total[h]
                struck = counted * box_table[taken, h, pl.ds(y0, n), :]
                mass = mass + jnp.sum(counted.reshape(n // 8, 8, LANES), axis=0)
                hit = hit + jnp.sum(struck.reshape(n // 8, 8, LANES), axis=0)
        return mass, hit

    zero = jnp.zeros((8, LANES), jnp.float32)
    sums = lax.fori_loop(2, bx - 2, functools.partial(finish, middle), (zero, zero), unroll=2)
    scale_halo(last)
    for x0 in (0, bx - 2):
        sums = lax.fori_loop(x0, x0 + 2, functools.partial(finish, whole), sums)
    edges = functools.partial(finish, [(0, 8), (by - 8, 8)])
    mass, hit = lax.fori_loop(2, bx - 2, edges, sums, unroll=4)

    row8 = lax.broadcasted_iota(jnp.int32, (8, LANES), 0)
    red_near[near_me] = jnp.where(
        row8 == 0,
        jnp.sum(mass, axis=0, keepdims=True),
        jnp.where(row8 == 1, jnp.sum(hit, axis=0, keepdims=True), 0.0),
    )

    def share_copy(ref, size, mine, send, recv, device, step, slot):
        return pltpu.make_async_remote_copy(
            src_ref=ref.at[mine],
            dst_ref=ref.at[slot],
            send_sem=send.at[step],
            recv_sem=recv.at[step],
            device_id=device(lax.rem(mine + step, size)),
            device_id_type=MESH,
        )

    def share(*group):
        ref, size, mine = group[:3]
        for step in range(1, size):
            share_copy(*group, step, mine).start()
        for step in range(1, size):
            share_copy(*group, step, lax.rem(mine + size - step, size)).wait_recv()
        total = ref[0]
        for slot in range(1, size):
            total = total + ref[slot]
        return total

    near = (red_near, near_size, near_me, nsend_sem, nrecv_sem, near_device)
    far = (red_far, far_size, far_me, fsend_sem, frecv_sem, far_device)
    red_far[far_me] = share(*near)
    total = share(*far)
    cells = float(extents[0] * extents[1] * extents[2])
    summary[0] = jnp.sum(total[1:2]) * jnp.float32(1.0 / cells)
    summary[1] = jnp.sum(total[0:1]) * jnp.float32(1.0 / cells)

    for step in range(1, near_size):
        share_copy(*near, step, near_me).wait_send()
    for step in range(1, far_size):
        share_copy(*far, step, far_me).wait_send()
    for k in range(STEPS):
        for way in range(8):

            @pl.when(exists[way])
            def _():
                halo_copy(k, way).wait_send()


def body(nx, ny, density, reaction_rates, state_changes, target_box, truncation):
    bx, by, nz = density.shape
    reactions = state_changes.shape[0]
    yp = by + 2 * PAD
    f32 = jnp.float32
    vmem = lambda *shape: pltpu.VMEM(shape, f32)
    dma = pltpu.SemaphoreType.DMA
    occupancy, summary = pl.pallas_call(
        functools.partial(kernel, nx, ny, bx, by, reactions),
        out_shape=(
            pltpu.VMEM((bx * by, nz), f32),
            jax.ShapeDtypeStruct((2,), f32),
        ),
        in_specs=[pl.BlockSpec(memory_space=pl.ANY)]
        + [pl.BlockSpec(memory_space=pltpu.SMEM)] * 4,
        out_specs=(
            pl.BlockSpec(memory_space=pltpu.VMEM),
            pl.BlockSpec(memory_space=pltpu.SMEM),
        ),
        scratch_shapes=[
            vmem(STEPS, 2, bx * by, LANES),
            vmem(10 * (bx + 4) * yp, LANES),
            vmem(2, bx * by, LANES),
            pltpu.VMEM((GROUP * by, 4 * LANES), jnp.bfloat16),
            pltpu.VMEM((len(MOVED), 4 * LANES, 2 * LANES), jnp.bfloat16),
            vmem(reactions, by, LANES),
            vmem(reactions, by, LANES),
            vmem(2, 2, by, LANES),
            vmem(2, 2, by, LANES),
            vmem(STEPS, 2, 2, 2 * by, LANES),
            vmem(STEPS, 2, 4 * bx, LANES),
            vmem(STEPS, 4, 2, 8, LANES),
            vmem(STEPS, 2, 4 * bx, LANES),
            vmem(STEPS, 4, 2, 8, LANES),
            vmem(ny, 8, LANES),
            vmem(nx, 8, LANES),
            dma((2,)),
            dma((STEPS, 8)),
            dma((STEPS, 8)),
            dma((ny,)),
            dma((ny,)),
            dma((nx,)),
            dma((nx,)),
        ],
        compiler_params=pltpu.CompilerParams(
            collective_id=0, has_side_effects=True, vmem_limit_bytes=54 * 1024 * 1024
        ),
    )(density.reshape(bx * by, nz), reaction_rates, state_changes.T, target_box, truncation)
    return occupancy.reshape(bx, by, nz), summary


def solution(mesh):
    placed = (P("gx", "gy", None), P(), P(), P(), P())
    return jax.shard_map(
        functools.partial(body, mesh.shape["gx"], mesh.shape["gy"]),
        mesh=mesh,
        in_specs=placed,
        out_specs=(P("gx", "gy", None), P()),
        check_vma=False,
    )
```

```python
import functools
import math

import jax
import jax.numpy as jnp
from jax import lax
from jax.experimental import pallas as pl
from jax.experimental.pallas import tpu as pltpu
from jax.sharding import PartitionSpec as P

STEPS = 4
mean_jumps = 8.0
headroom = 1.05
series_length = 40
TABLE = [
    math.exp(-mean_jumps) * mean_jumps**k / math.factorial(k) for k in range(series_length)
]
MESH = pl.DeviceIdType.MESH
LANES = 128
GROUP = 8
MOVED = (1, 2)
PAD = 8
MOVES = [(-1, 0), (1, 0), (0, -1), (0, 1), (-1, -1), (-1, 1), (1, -1), (1, 1)]
BACK = [1, 0, 3, 2, 7, 6, 5, 4]


def quadratic(order, extent):
    zero = jnp.float32(0.0)
    return (
        jnp.where(order == 0, jnp.float32(1.0), zero),
        jnp.where(order == 1, jnp.float32(1.0 / extent), zero),
        jnp.where(order == 2, jnp.float32(1.0 / (extent * extent)), zero),
    )


def evaluate(coefficients, m):
    c0, c1, c2 = coefficients
    return c0 + c1 * m + c2 * (m * (m - 1.0))


def kernel(
    nx, ny, bx, by, reactions,
    density, rates, changes, box, truncation,
    occupancy, summary,
    p, s, d, parts, movers, shifted_b, plain_b, self_c, free_table, box_table,
    recv_x, recv_y, recv_c, send_y, send_c, red_near, red_far,
    load_sem, send_sem, recv_sem, nsend_sem, nrecv_sem, fsend_sem, frecv_sem,
):
    me_x, me_y = lax.axis_index("gx"), lax.axis_index("gy")
    anchor_x, anchor_y = me_x * bx, me_y * by
    extents = (nx * bx, ny * by, 2 * LANES)
    yp = by + 2 * PAD
    plane = (bx + 4) * yp

    def present(move):
        px, py = me_x + move[0], me_y + move[1]
        return (px >= 0) & (px < nx) & (py >= 0) & (py < ny)

    exists = [present(move) for move in MOVES]

    loads = [
        pltpu.make_async_copy(
            density.at[:, pl.ds(h * LANES, LANES)], p.at[0, h], load_sem.at[h]
        )
        for h in range(2)
    ]
    for load in loads:
        load.start()

    barrier = pltpu.get_barrier_semaphore()

    def greet(px, py):
        pl.semaphore_signal(barrier, inc=1, device_id=(px, py), device_id_type=MESH)

    inner_x, outer_y = 4, 2
    outer_x, inner_y = nx // inner_x, ny // outer_y
    near_size, far_size = inner_x * outer_y, outer_x * inner_y
    near_me = (me_x % inner_x) * outer_y + me_y // inner_y
    far_me = (me_x // inner_x) * inner_y + me_y % inner_y

    def near_device(other):
        return (
            (me_x // inner_x) * inner_x + other // outer_y,
            (other % outer_y) * inner_y + me_y % inner_y,
        )

    def far_device(other):
        return (
            (other // inner_y) * inner_x + me_x % inner_x,
            (me_y // inner_y) * inner_y + other % inner_y,
        )

    for size, mine, device in ((near_size, near_me, near_device), (far_size, far_me, far_device)):

        @pl.loop(1, size)
        def _(step):
            greet(*device((mine + step) % size))

    others = jnp.int32(0)
    for way in range(8):
        px, py = me_x + MOVES[way][0], me_y + MOVES[way][1]
        is_near = (px // inner_x == me_x // inner_x) & (py % inner_y == me_y % inner_y)
        is_far = (px % inner_x == me_x % inner_x) & (py // inner_y == me_y // inner_y)
        alone = exists[way] & jnp.logical_not(is_near | is_far)
        others = others + alone.astype(jnp.int32)

        @pl.when(alone)
        def _():
            greet(px, py)

    for k in range(STEPS):
        for c in range(4):
            send_c[k, c] = jnp.zeros((2, 8, LANES), jnp.float32)

    def halo_copy(k, way):
        px, py = me_x + MOVES[way][0], me_y + MOVES[way][1]
        land = BACK[way]
        if way < 2:
            start = 0 if way == 0 else (bx - 2) * by
            source = p.at[k, :, pl.ds(start, 2 * by), :]
            target = recv_x.at[k, land]
        elif way < 4:
            source = send_y.at[k, way - 2]
            target = recv_y.at[k, land - 2]
        else:
            source = send_c.at[k, way - 4]
            target = recv_c.at[k, land - 4]
        return pltpu.make_async_remote_copy(
            src_ref=source,
            dst_ref=target,
            send_sem=send_sem.at[k, way],
            recv_sem=recv_sem.at[k, land],
            device_id=(px, py),
            device_id_type=MESH,
        )

    def arrived(k, way):
        return pltpu.make_async_remote_copy(
            src_ref=(p.at[k, :, pl.ds(0, 2 * by), :] if way < 2 else send_y.at[k, way - 2] if way < 4 else send_c.at[k, way - 4]),
            dst_ref=(recv_x.at[k, way] if way < 2 else recv_y.at[k, way - 2] if way < 4 else recv_c.at[k, way - 4]),
            send_sem=send_sem.at[k, way],
            recv_sem=recv_sem.at[k, way],
            device_id=(me_x + MOVES[way][0], me_y + MOVES[way][1]),
            device_id_type=MESH,
        )

    def send_faces(k, ways):
        for way in ways:

            @pl.when(exists[way])
            def _():
                halo_copy(k, way).start()

    def pack(k):
        for side in range(2):
            for j in range(2):
                y = j if side == 0 else by - 2 + j
                for h in range(2):
                    send_y[k, side, pl.ds((j * 2 + h) * bx, bx), :] = p[k, h, pl.ds(y, bx, stride=by), :]
        for c in range(4):
            x0 = 0 if MOVES[4 + c][0] < 0 else bx - 2
            y0 = 0 if MOVES[4 + c][1] < 0 else by - 2
            for h in range(2):
                for x in range(2):
                    send_c[k, c, h, pl.ds(2 * x, 2), :] = p[k, h, pl.ds((x0 + x) * by + y0, 2), :]

    for load in loads:
        load.wait()
    pl.semaphore_wait(barrier, near_size - 1 + far_size - 1 + others)
    send_faces(0, (0, 1))
    pack(0)
    send_faces(0, range(2, 8))

    order = [[jnp.maximum(-changes[a, r], 0) for a in range(3)] for r in range(reactions)]
    phi = [[quadratic(order[r][a], float(extents[a])) for a in range(3)] for r in range(reactions)]
    corner = None
    for r in range(reactions):
        term = rates[r]
        for a in range(3):
            term = term * evaluate(phi[r][a], jnp.float32(extents[a] - 1))
        corner = term if corner is None else corner + term
    inverse_rate = 1.0 / jnp.full((8, LANES), headroom * corner, jnp.float32)
    inverse_rate = inverse_rate[0:1]
    tails = []
    for which in range(2):
        tail = jnp.float32(0.0)
        for k in range(STEPS + 1, series_length):
            tail = tail + jnp.where(k <= truncation[which], jnp.float32(TABLE[k]), jnp.float32(0.0))
        tails.append(tail)
    offsets = [
        (changes[2, r] + 2) * (2 * plane) + (2 - changes[0, r]) * yp + (PAD - changes[1, r])
        for r in range(reactions)
    ]

    def within(count, a):
        return (count >= box[0, a]) & (count < box[1, a])

    def along_x(x_local, move):
        out = []
        for r in range(reactions):
            count = anchor_x + x_local
            if move:
                count = count - changes[0, r]
            out.append(rates[r] * evaluate(phi[r][0], count.astype(jnp.float32)))
        return out

    def lanes(rows):
        return lax.broadcasted_iota(jnp.int32, (rows, LANES), 1)

    z_count = [lanes(1) + h * LANES for h in range(2)]
    z_float = [z.astype(jnp.float32) for z in z_count]
    z_box = [within(z, 2).astype(jnp.float32) for z in z_count]
    z_one = [z * (1.0 / extents[2]) for z in z_float]
    z_two = [z * (z - 1.0) * (1.0 / extents[2] ** 2) for z in z_float]

    z_two_after = [(z + 2.0) * (z + 1.0) * (1.0 / extents[2] ** 2) for z in z_float]
    source = lax.broadcasted_iota(jnp.int32, (4 * LANES, 2 * LANES), 0) & (2 * LANES - 1)
    target = lax.broadcasted_iota(jnp.int32, (4 * LANES, 2 * LANES), 1)
    for m, v in enumerate(MOVED):
        weight = source.astype(jnp.float32) * (1.0 / extents[2]) if v == -1 else jnp.float32(1.0)
        movers[m] = jnp.where(target - source == v, weight, 0.0).astype(jnp.bfloat16)

    rows = lax.broadcasted_iota(jnp.int32, (by, LANES), 0) + anchor_y
    for r in range(reactions):
        shifted_b[r] = evaluate(phi[r][1], (rows - changes[1, r]).astype(jnp.float32))
    y_box = within(rows, 1).astype(jnp.float32)
    for h in range(2):
        inside = y_box * z_box[h]
        free_table[0, h] = jnp.broadcast_to(inverse_rate, (by, LANES))
        free_table[1, h] = inverse_rate * (1.0 - inside)
        box_table[0, h] = jnp.zeros((by, LANES), jnp.float32)
        box_table[1, h] = inside

    for way in range(8):

        @pl.when(jnp.logical_not(exists[way]))
        def _():
            for k in range(STEPS):
                if way < 2:
                    recv_x[k, way] = jnp.zeros((2, 2 * by, LANES), jnp.float32)
                elif way < 4:
                    recv_y[k, way - 2] = jnp.zeros((4 * bx, LANES), jnp.float32)
                else:
                    recv_c[k, way - 4] = jnp.zeros((2, 8, LANES), jnp.float32)

    def shifts(c0, c1, f0, f1, skip=()):
        lane = lanes(c0.shape[0])
        zero = jnp.zeros_like(c0)
        a0, a1 = c0 * f0, c1 * f1
        out = []
        for v in range(-2, 3):
            if v == 0:
                out.append((a0, a1))
                continue
            if v in skip:
                out.append(None)
                continue
            if v > 0:
                t0, t1 = pltpu.roll(a0, v, 1), pltpu.roll(a1, v, 1)
                out.append((jnp.where(lane < v, zero, t0), jnp.where(lane < v, t0, t1)))
            else:
                factor = z_one if v == -1 else z_two
                t0 = pltpu.roll(a0 * factor[0], LANES + v, 1)
                t1 = pltpu.roll(a1 * factor[1], LANES + v, 1)
                edge = lane >= LANES + v
                out.append((jnp.where(edge, t1, t0), jnp.where(edge, zero, t1)))
        return out

    chunk = min(64, by)

    def scale_plane(x_local, load, slot=None):
        taken = within(anchor_x + x_local, 0).astype(jnp.int32)
        for y0 in range(0, by, chunk):
            c0, c1 = load(0, y0), load(1, y0)
            f0 = free_table[taken, 0, pl.ds(y0, chunk), :]
            f1 = free_table[taken, 1, pl.ds(y0, chunk), :]
            row = pl.multiple_of((x_local + 2) * yp + (PAD + y0), 8)
            for v, pair in enumerate(shifts(c0, c1, f0, f1, MOVED if slot is not None else ())):
                if pair is None:
                    continue
                for h in range(2):
                    s[pl.ds((v * 2 + h) * plane + row, chunk), :] = pair[h]
                if v == 2 and slot is not None:
                    for h in range(2):
                        high = pair[h].astype(jnp.bfloat16)
                        low = (pair[h] - high.astype(jnp.float32)).astype(jnp.bfloat16)
                        here = pl.ds(slot * by + y0, chunk)
                        parts[here, pl.ds(h * LANES, LANES)] = high
                        parts[here, pl.ds((2 + h) * LANES, LANES)] = low

    def move_planes(xs):
        for m, v in enumerate(MOVED):
            moved = jnp.dot(
                parts[pl.ds(0, len(xs) * by), :], movers[m], preferred_element_type=jnp.float32
            )
            for h in range(2):
                for i, x in enumerate(xs):
                    value = moved[i * by : (i + 1) * by, h * LANES : (h + 1) * LANES]
                    if v == -2:
                        value = value * z_two_after[h]
                    row = pl.multiple_of((x + 2) * yp + PAD, 8)
                    s[pl.ds(((v + 2) * 2 + h) * plane + row, by), :] = value

    def scale_own(k):
        @pl.loop(0, bx // GROUP)
        def _(group):
            first = group * GROUP
            for i in range(GROUP):
                base = pl.multiple_of((first + i) * by, 8)
                scale_plane(first + i, lambda h, y0: p[k, h, pl.ds(base + y0, chunk), :], i)
            move_planes([first + i for i in range(GROUP)])

    def await_halo(k, ways):
        for way in ways:

            @pl.when(exists[way])
            def _():
                arrived(k, way).wait_recv()

    def scale_halo(k):
        await_halo(k, range(2, 8))
        x_row = lax.broadcasted_iota(jnp.int32, (bx, LANES), 0) + anchor_x
        x_box = within(x_row, 0).astype(jnp.float32)
        for way in range(2, 4):
            for j in range(2):
                y = j - 2 if way == 2 else by + j
                inside = x_box * within(anchor_y + y, 1).astype(jnp.float32)
                c0 = recv_y[k, way - 2, pl.ds((j * 2) * bx, bx), :]
                c1 = recv_y[k, way - 2, pl.ds((j * 2 + 1) * bx, bx), :]
                f0 = inverse_rate * (1.0 - inside * z_box[0])
                f1 = inverse_rate * (1.0 - inside * z_box[1])
                for v, pair in enumerate(shifts(c0, c1, f0, f1)):
                    for h in range(2):
                        s[pl.ds((v * 2 + h) * plane + 2 * yp + PAD + y, bx, stride=yp), :] = pair[h]
        small = lax.broadcasted_iota(jnp.int32, (8, LANES), 0)
        for way in range(4, 8):
            x0 = -2 if MOVES[way][0] < 0 else bx
            y0 = -2 if MOVES[way][1] < 0 else by
            inside = (
                within(anchor_x + x0 + (small >> 1), 0) & within(anchor_y + y0 + (small & 1), 1)
            ).astype(jnp.float32)
            c0 = recv_c[k, way - 4, 0]
            c1 = recv_c[k, way - 4, 1]
            f0 = inverse_rate * (1.0 - inside * z_box[0])
            f1 = inverse_rate * (1.0 - inside * z_box[1])
            for v, pair in enumerate(shifts(c0, c1, f0, f1)):
                for h in range(2):
                    for x in range(2):
                        row = (v * 2 + h) * plane + (x0 + x + 2) * yp + PAD + y0
                        s[pl.ds(row, 2), :] = pair[h][2 * x : 2 * x + 2]
        await_halo(k, range(2))
        places = [(way, i) for way in range(2) for i in range(2)]
        xs = [i - 2 if way == 0 else bx + i for way, i in places]
        for slot, (way, i) in enumerate(places):
            scale_plane(
                jnp.int32(xs[slot]),
                lambda h, y0: recv_x[k, way, h, pl.ds(i * by + y0, chunk), :],
                slot,
            )
        move_planes(xs)

    def advance(k, x, factors, y0, n):
        base = pl.multiple_of(x * by + y0, 8)
        total = [p[k, h, pl.ds(base, n), :] * d[h, pl.ds(base, n), :] for h in range(2)]
        for r in range(reactions):
            along = factors[r] * shifted_b[r, pl.ds(y0, n), :]
            for h in range(2):
                row = offsets[r] + (x * yp + (h * plane + y0))
                total[h] = total[h] + along * s[pl.ds(row, n), :]
        return base, total

    def advance_to(k, x, spans):
        factors = along_x(x, True)
        for y0, n in spans:
            base, total = advance(k, x, factors, y0, n)
            for h in range(2):
                p[k + 1, h, pl.ds(base, n), :] = total[h]

    half = by // 2
    whole = [(0, half), (half, half)]
    inner = (by - 16) // 2
    middle = [(8, inner), (8 + inner, inner)]

    def advance_middle(k):
        @pl.loop(2, bx - 2, unroll=2)
        def _(x):
            advance_to(k, x, middle)

    def self_term():
        def pick(index, values):
            out = jnp.zeros(index.shape, jnp.float32)
            for r, value in enumerate(values):
                out = jnp.where(index == r, value, out)
            return out

        column = lanes(1)
        reaction, piece = column & 7, column >> 4
        along = [
            tuple(pick(reaction, [phi[r][a][i] for r in range(reactions)]) for i in range(3))
            for a in range(2)
        ]
        rate = jnp.where(column < 48, pick(reaction, [rates[r] for r in range(reactions)]), 0.0)
        plain_b[...] = evaluate(along[1], rows.astype(jnp.float32))
        row = lax.broadcasted_iota(jnp.int32, (LANES, LANES), 0)
        for h in range(2):
            factor = pick(row & 7, [evaluate(phi[r][2], z_float[h]) for r in range(reactions)])
            coarse = factor.astype(jnp.bfloat16).astype(jnp.float32)
            factor = jnp.where((row >> 3) & 1 == 0, coarse, factor - coarse)
            self_c[:, pl.ds(h * LANES, LANES)] = factor.astype(jnp.bfloat16)

        @pl.loop(0, bx // GROUP)
        def _(group):
            first = group * GROUP
            for i in range(GROUP):
                count = (anchor_x + first + i).astype(jnp.float32)
                value = (rate * evaluate(along[0], count)) * plain_b[...]
                high = value.astype(jnp.bfloat16).astype(jnp.float32)
                rest = value - high
                middle_part = rest.astype(jnp.bfloat16).astype(jnp.float32)
                part = jnp.where(piece == 0, high, jnp.where(piece == 1, middle_part, rest - middle_part))
                parts[pl.ds(i * by, by), pl.ds(0, LANES)] = part.astype(jnp.bfloat16)
            total = jnp.dot(
                parts[:, pl.ds(0, LANES)], self_c[...], preferred_element_type=jnp.float32
            )
            for i in range(GROUP):
                taken = within(anchor_x + first + i, 0).astype(jnp.int32)
                base = pl.multiple_of((first + i) * by, 8)
                for h in range(2):
                    a0 = total[i * by : (i + 1) * by, h * LANES : (h + 1) * LANES]
                    d[h, pl.ds(base, by), :] = 1.0 - a0 * free_table[taken, h]

    scale_own(0)
    self_term()
    advance_middle(0)

    @pl.loop(0, STEPS - 1)
    def _(k):
        scale_halo(k)
        for x0 in (0, bx - 2):

            @pl.loop(x0, x0 + 2)
            def _(x):
                advance_to(k, x, whole)

        send_faces(k + 1, (0, 1))

        @pl.loop(2, bx - 2, unroll=4)
        def _(x):
            advance_to(k, x, [(0, 8), (by - 8, 8)])

        pack(k + 1)
        send_faces(k + 1, range(2, 8))

        scale_own(k + 1)

        @pl.when(k + 1 < STEPS - 1)
        def _():
            advance_middle(k + 1)

    last = STEPS - 1
    weights = [jnp.float32(TABLE[k]) for k in range(STEPS + 1)]
    weight_density = weights[STEPS] + tails[0]
    weight_total = weights[STEPS] + tails[1]

    def finish(spans, x, carry):
        mass, hit = carry
        factors = along_x(x, True)
        taken = within(anchor_x + x, 0).astype(jnp.int32)
        for y0, n in spans:
            base, total = advance(last, x, factors, y0, n)
            for h in range(2):
                earlier = weights[0] * p[0, h, pl.ds(base, n), :]
                for k in range(1, STEPS):
                    earlier = earlier + weights[k] * p[k, h, pl.ds(base, n), :]
                occupancy[pl.ds(base, n), pl.ds(h * LANES, LANES)] = earlier + weight_density * total[h]
                counted = earlier + weight_total * total[h]
                struck = counted * box_table[taken, h, pl.ds(y0, n), :]
                mass = mass + jnp.sum(counted.reshape(n // 8, 8, LANES), axis=0)
                hit = hit + jnp.sum(struck.reshape(n // 8, 8, LANES), axis=0)
        return mass, hit

    zero = jnp.zeros((8, LANES), jnp.float32)
    sums = lax.fori_loop(2, bx - 2, functools.partial(finish, middle), (zero, zero), unroll=2)
    scale_halo(last)
    for x0 in (0, bx - 2):
        sums = lax.fori_loop(x0, x0 + 2, functools.partial(finish, whole), sums)
    edges = functools.partial(finish, [(0, 8), (by - 8, 8)])
    mass, hit = lax.fori_loop(2, bx - 2, edges, sums, unroll=4)

    row8 = lax.broadcasted_iota(jnp.int32, (8, LANES), 0)
    red_near[near_me] = jnp.where(
        row8 == 0,
        jnp.sum(mass, axis=0, keepdims=True),
        jnp.where(row8 == 1, jnp.sum(hit, axis=0, keepdims=True), 0.0),
    )

    def share_copy(ref, size, mine, send, recv, device, step, slot):
        return pltpu.make_async_remote_copy(
            src_ref=ref.at[mine],
            dst_ref=ref.at[slot],
            send_sem=send.at[step],
            recv_sem=recv.at[step],
            device_id=device(lax.rem(mine + step, size)),
            device_id_type=MESH,
        )

    def share(*group):
        ref, size, mine = group[:3]
        for step in range(1, size):
            share_copy(*group, step, mine).start()
        for step in range(1, size):
            share_copy(*group, step, lax.rem(mine + size - step, size)).wait_recv()
        total = ref[0]
        for slot in range(1, size):
            total = total + ref[slot]
        return total

    near = (red_near, near_size, near_me, nsend_sem, nrecv_sem, near_device)
    far = (red_far, far_size, far_me, fsend_sem, frecv_sem, far_device)
    red_far[far_me] = share(*near)
    total = share(*far)
    cells = float(extents[0] * extents[1] * extents[2])
    summary[0] = jnp.sum(total[1:2]) * jnp.float32(1.0 / cells)
    summary[1] = jnp.sum(total[0:1]) * jnp.float32(1.0 / cells)

    for step in range(1, near_size):
        share_copy(*near, step, near_me).wait_send()
    for step in range(1, far_size):
        share_copy(*far, step, far_me).wait_send()
    for k in range(STEPS):
        for way in range(8):

            @pl.when(exists[way])
            def _():
                halo_copy(k, way).wait_send()


def body(nx, ny, density, reaction_rates, state_changes, target_box, truncation):
    bx, by, nz = density.shape
    reactions = state_changes.shape[0]
    yp = by + 2 * PAD
    f32 = jnp.float32
    vmem = lambda *shape: pltpu.VMEM(shape, f32)
    dma = pltpu.SemaphoreType.DMA
    occupancy, summary = pl.pallas_call(
        functools.partial(kernel, nx, ny, bx, by, reactions),
        out_shape=(
            pltpu.VMEM((bx * by, nz), f32),
            jax.ShapeDtypeStruct((2,), f32),
        ),
        in_specs=[pl.BlockSpec(memory_space=pl.ANY)]
        + [pl.BlockSpec(memory_space=pltpu.SMEM)] * 4,
        out_specs=(
            pl.BlockSpec(memory_space=pltpu.VMEM),
            pl.BlockSpec(memory_space=pltpu.SMEM),
        ),
        scratch_shapes=[
            vmem(STEPS, 2, bx * by, LANES),
            vmem(10 * (bx + 4) * yp, LANES),
            vmem(2, bx * by, LANES),
            pltpu.VMEM((GROUP * by, 4 * LANES), jnp.bfloat16),
            pltpu.VMEM((len(MOVED), 4 * LANES, 2 * LANES), jnp.bfloat16),
            vmem(reactions, by, LANES),
            vmem(by, LANES),
            pltpu.VMEM((LANES, 2 * LANES), jnp.bfloat16),
            vmem(2, 2, by, LANES),
            vmem(2, 2, by, LANES),
            vmem(STEPS, 2, 2, 2 * by, LANES),
            vmem(STEPS, 2, 4 * bx, LANES),
            vmem(STEPS, 4, 2, 8, LANES),
            vmem(STEPS, 2, 4 * bx, LANES),
            vmem(STEPS, 4, 2, 8, LANES),
            vmem(ny, 8, LANES),
            vmem(nx, 8, LANES),
            dma((2,)),
            dma((STEPS, 8)),
            dma((STEPS, 8)),
            dma((ny,)),
            dma((ny,)),
            dma((nx,)),
            dma((nx,)),
        ],
        compiler_params=pltpu.CompilerParams(
            collective_id=0, has_side_effects=True, vmem_limit_bytes=54 * 1024 * 1024
        ),
    )(density.reshape(bx * by, nz), reaction_rates, state_changes.T, target_box, truncation)
    return occupancy.reshape(bx, by, nz), summary


def solution(mesh):
    placed = (P("gx", "gy", None), P(), P(), P(), P())
    return jax.shard_map(
        functools.partial(body, mesh.shape["gx"], mesh.shape["gy"]),
        mesh=mesh,
        in_specs=placed,
        out_specs=(P("gx", "gy", None), P()),
        check_vma=False,
    )
```
